32 devices in a mesh: gz: 16 (over z, y, core), xy: 2 (over x).
Axes of the slice: x: 2, y: 2, z: 4, core: 2. Of those that a mesh axis runs over, the one named last changes fastest.
Arguments:
- fields: float32 [2, 1024, 64, 256], P(None, 'gz', 'xy'), may hold values from -64 to 64, as said below
- threshold: float32 [2], replicated, may hold values from 0.1 to 0.6
Outputs:
- detail_one: float32 [2, 512, 64, 256], P(None, 'gz', 'xy')
- detail_two: float32 [2, 256, 64, 256], P(None, 'gz', 'xy')
- detail_three: float32 [2, 128, 64, 256], P(None, 'gz', 'xy')
- detail_four: float32 [2, 64, 64, 256], P(None, 'gz', 'xy')
- detail_five: float32 [2, 32, 64, 256], P(None, 'gz', 'xy')
- coarse: float32 [2, 32, 64, 256], P(None, 'gz', 'xy')
- band_energy: float32 [2, 6], replicated
The draws below stay inside these ranges and needn't reach their ends.
Inputs may be any that keep to these rules, and one draw needn't show every extreme that they name: Finite values; the spread of the fields varies over the grid.
All inputs are finite; a program needn't handle non-finite values.
Results may differ from the reference program's by a relative error of at most 0.00002.
Values sent between devices are 32-bit elements; how exact they have to be, the bound alone decides.
A program may use at most 64 MiB of HBM per device.

```python
import jax
import jax.numpy as jnp

NY = 256
NZ = 1024
NX = 64


def draw_fields(key, part):
    depth = jnp.arange(NZ, dtype=jnp.float32) / NZ
    across = jnp.arange(NX, dtype=jnp.float32) / NX
    scale = jnp.exp(jnp.log(4.0) * depth)[:, None, None] * (1.0 + across)[None, :, None]
    noise = jax.random.normal(jax.random.fold_in(key, 13), (2, NZ, NX, NY), jnp.float32)
    values = noise * scale[None]
    return values.astype(jnp.float32)


def setup_inputs(seed: int = 0) -> dict:
    key_of = jax.random.split(jax.random.key(seed), 3)
    return {
        "fields": draw_fields(jax.random.fold_in(key_of[2], 71), 0),
        "threshold": jnp.clip(jax.random.uniform(key_of[1], (2,), jnp.float32, 0.1, 0.6), 0.1, 0.6),
    }


ALPHA = -1.586134342059924
BETA = -0.052980118572961
GAMMA = 0.882911075530934
DELTA = 0.443506852043971
KAPPA = 1.230174104914001
SQRT_TWO = 1.4142135623730951


def right_of(evens):
    return jnp.concatenate([evens[:, 1:], evens[:, -1:]], axis=1)


def left_of(odds):
    return jnp.concatenate([odds[:, :1], odds[:, :-1]], axis=1)


def one_level(values):
    half = values.shape[1] // 2
    paired = values.reshape(values.shape[0], half, 2, values.shape[2], values.shape[3])
    evens = paired[:, :, 0]
    odds = paired[:, :, 1]
    odds = odds + ALPHA * (evens + right_of(evens))
    evens = evens + BETA * (left_of(odds) + odds)
    odds = odds + GAMMA * (evens + right_of(evens))
    evens = evens + DELTA * (left_of(odds) + odds)
    return evens * (SQRT_TWO / KAPPA), odds * (KAPPA / SQRT_TWO)


def shrink(band, limit):
    return band - jnp.clip(band, -limit, limit)


def reference(fields, threshold):
    limit = threshold.reshape(2, 1, 1, 1)
    bands = []
    approx = fields
    for level in range(5):
        approx, detail = one_level(approx)
        bands.append(shrink(detail, limit))
    bands.append(shrink(approx, limit))
    energy = jnp.stack([jnp.sum(band * band, axis=(1, 2, 3)) / (band.shape[1] * band.shape[2] * band.shape[3]) for band in bands], axis=1)
    return (bands[0], bands[1], bands[2], bands[3], bands[4], bands[5], energy)
```

```python
import functools

import jax
import jax.numpy as jnp
from jax import lax
from jax.experimental import pallas as pl
from jax.experimental.pallas import tpu as pltpu
from jax.sharding import PartitionSpec as P

ALPHA = -1.586134342059924
BETA = -0.052980118572961
GAMMA = 0.882911075530934
DELTA = 0.443506852043971
KAPPA = 1.230174104914001
SQRT_TWO = 1.4142135623730951
LEVELS = 5
MESH = pl.DeviceIdType.MESH
SUB = 8
ROWS = 16


def plus(*terms):
    terms = [term for term in terms if term is not None]
    return functools.reduce(lambda x, y: x + y, terms) if terms else None


def times(factor, value):
    return None if value is None else factor * value


def head_states(entry):
    s_head, d_head, s_after = (entry(j) for j in range(3))
    d_lifted = plus(d_head, times(ALPHA, plus(s_head, s_after)))
    return s_head, plus(s_head, times(BETA, d_lifted))


def tail_states(entry):
    s_prev, d_prev, s_tail, d_tail = (entry(j) for j in range(-4, 0))
    d_lifted = plus(d_prev, times(ALPHA, plus(s_prev, s_tail)))
    return plus(d_tail, times(ALPHA, s_tail)), plus(s_tail, times(BETA, d_lifted))


def echo(entry, states, head):
    reach = range(-1, 4) if head else range(-4, 1)
    inside = (lambda j: j >= 0) if head else (lambda j: j < 0)
    s = {j: entry(2 * j) for j in reach if inside(j)}
    d = {j: entry(2 * j + 1) for j in reach if inside(j)}
    if not head:
        s[0] = states[0]
    d1, s1, d2, s2 = {}, {}, {}, {}
    for j in reach:
        if inside(j):
            d1[j] = plus(d.get(j), times(ALPHA, plus(s.get(j), s.get(j + 1))))
    if head:
        d1[-1] = plus(states[0], times(ALPHA, s[0]))
    for j in reach:
        if inside(j):
            s1[j] = plus(s.get(j), times(BETA, plus(d1.get(j - 1), d1.get(j))))
    beyond = -1 if head else 0
    s1[beyond] = plus(states[1], times(BETA, d1[-1]))
    for j in range(-1, 4) if head else range(-4, 0):
        d2[j] = plus(d1.get(j), times(GAMMA, plus(s1.get(j), s1.get(j + 1))))
    for j in reach:
        if inside(j):
            s2[j] = plus(s1.get(j), times(DELTA, plus(d2.get(j - 1), d2.get(j))))
    return {j: times(SQRT_TWO / KAPPA, value) for j, value in s2.items() if value is not None}


HEAD_TOUCHED = ((1, 2), (2, 3), (3, 4))
TAIL_TOUCHED = ((2, 2), (3, 3), (3, 3))
TRAIL_HEAD = (0, 2, 3, 4)
TRAIL_TAIL = (0, 2, 3, 3)


def kernel(
    gz_count,
    xy_count,
    threshold_hbm,
    fields_ref,
    *refs,
):
    outs = refs[: LEVELS + 1]
    energy_ref = refs[LEVELS + 1]
    inputs = refs[LEVELS + 2 : 2 * LEVELS + 2]
    (slow_send, slow_recv, fast_send, fast_recv, bias, trail, acc, e_send_buf, e_recv_buf) = refs[
        2 * LEVELS + 2 : 2 * LEVELS + 11
    ]
    (
        threshold_ref,
        in_sem,
        edge_sem,
        slow_send_sem,
        slow_recv_sem,
        fast_send_sem,
        fast_recv_sem,
        e_send_sem,
        e_recv_sem,
        limit_sem,
        ready_sem,
    ) = refs[2 * LEVELS + 11 :]
    field_count, layers, width, _ = fields_ref.shape
    per_field = width // ROWS
    chunks = field_count * per_field
    devices = gz_count * xy_count
    stages = (gz_count - 1).bit_length()

    gz = lax.axis_index("gz")
    xy = lax.axis_index("xy")
    me = gz * xy_count + xy
    first = gz == 0
    last = gz == gz_count - 1
    even = lax.rem(gz, 2) == 0

    def wrapped(value, step, count):
        moved = value + step
        return jnp.where(moved >= count, moved - count, moved)

    def for_peers(act):
        for across in range(1, xy_count):
            act((gz, wrapped(xy, across, xy_count)))

        @pl.loop(1, gz_count)
        def _(along):
            for across in range(xy_count):
                act((wrapped(gz, along, gz_count), wrapped(xy, across, xy_count)))

    def for_both(step, act):
        @pl.when(gz >= step)
        def _():
            act(gz - step)

        @pl.when(gz < gz_count - step)
        def _():
            act(gz + step)

    def beside(step):
        return (gz >= step).astype(jnp.int32) + (gz < gz_count - step).astype(jnp.int32)

    barrier = pltpu.get_barrier_semaphore()

    def signal(sem, peer):
        pl.semaphore_signal(sem, inc=1, device_id=peer, device_id_type=MESH)

    for_both(1, lambda peer: signal(barrier, (peer, xy)))
    for across in range(1, xy_count):
        signal(barrier, (gz, wrapped(xy, across, xy_count)))

    def ready_signal(k):
        if k < stages:
            for_both(1 << k, lambda peer: signal(ready_sem.at[k], (peer, xy)))

    def ready_wait(k):
        if k < stages:
            pl.semaphore_wait(ready_sem.at[k], beside(1 << k))

    def place(c):
        return c // per_field, pl.multiple_of(lax.rem(c, per_field) * ROWS, ROWS)

    def edge_copy(side):
        part = pl.ds(0 if side == 0 else layers - 4, 4)
        return pltpu.make_async_copy(
            fields_ref.at[:, part], inputs[0].at[:, part], edge_sem.at[side]
        )

    def body_copy(c):
        f, row = place(c)
        where = (f, pl.ds(4, layers - 8), pl.ds(row, ROWS))
        return pltpu.make_async_copy(
            fields_ref.at[where], inputs[0].at[where], in_sem.at[c]
        )

    edge_copy(0).start()
    edge_copy(1).start()
    limit_copy = pltpu.make_async_copy(threshold_hbm, threshold_ref, limit_sem)
    limit_copy.start()

    @pl.loop(0, chunks)
    def _(c):
        body_copy(c).start()

    acc[...] = jnp.zeros_like(acc)

    def tiles(c):
        f, row = place(c)
        for t in range(ROWS // SUB):
            yield f, pl.ds(pl.multiple_of(row + t * SUB, SUB), SUB), pl.ds(t * SUB, SUB)

    def states_of(level, f, at, head):
        source = inputs[level]
        count = source.shape[1]
        make = head_states if head else tail_states
        return make(lambda j: source[f, j if j >= 0 else count + j, at])

    def put_states(buf, level, c, head):
        for f, at, to in tiles(c):
            one, two = states_of(level, f, at, head)
            buf[level, c, 0, to] = one
            buf[level, c, 1, to] = two

    def copy_of(send, recv, send_sem, recv_sem, level, c, peer):
        return pltpu.make_async_remote_copy(
            src_ref=send.at[level, c],
            dst_ref=recv.at[level, c],
            send_sem=send_sem.at[level, c],
            recv_sem=recv_sem.at[level, c],
            device_id={"gz": peer},
            device_id_type=MESH,
        )

    def lift(level, c, begin, end, low, high, emit_detail, emit_approx):
        source = inputs[level]
        half = source.shape[1] // 2
        final = level == LEVELS - 1
        limit = threshold_ref[c // per_field]

        def shrink(band):
            return band - jnp.minimum(jnp.maximum(band, -limit), limit)

        for f, at, to in tiles(c):
            evens = lambda i: source[f, 2 * i, at]
            odds = lambda i: source[f, 2 * i + 1, at]
            d1, s1, d2, sums = {}, {}, {}, {}

            def incoming(kind, which):
                if kind == "fast":
                    return fast_recv[level, c, which, to]
                if kind == "slow":
                    value = slow_recv[level, c, which, to]
                    return value + bias[c, which, to] if level else value
                return None

            def at_first(kind, mirrored, outer):
                return outer if kind == "fast" else jnp.where(first, mirrored, outer)

            def at_last(kind, mirrored, outer):
                outer = jnp.zeros_like(mirrored) if outer is None else outer
                return outer if kind == "fast" else jnp.where(last, mirrored, outer)

            def emit(kind, ref, i, value):
                band = shrink(value)
                ref[f, i, at] = band
                square = band * band
                sums[kind] = sums[kind] + square if kind in sums else square

            s = evens(begin)
            for i in range(begin, end + 1):
                if i < end:
                    if i + 1 < half:
                        s_next = evens(i + 1)
                    else:
                        s_next = at_last(high, s, incoming(high, 0))
                    d1[i] = odds(i) + ALPHA * (s + s_next)
                    if i == begin and low:
                        d1[i - 1] = at_first(low, d1[i], plus(incoming(low, 0), ALPHA * s))
                    if i - 1 in d1:
                        s1[i] = s + BETA * (d1[i - 1] + d1[i])
                    if i == begin and low:
                        s1[i - 1] = plus(incoming(low, 1), BETA * d1[i - 1])
                        d2[i - 1] = d1[i - 1] + GAMMA * (s1[i - 1] + s1[i])
                    s = s_next
                elif high:
                    s1[i] = at_last(high, s1[i - 1], plus(incoming(high, 1), BETA * d1[i - 1]))
                if i > begin and i - 1 in s1 and i in s1:
                    d2[i - 1] = d1[i - 1] + GAMMA * (s1[i - 1] + s1[i])
                    if i - 1 == begin and low:
                        d2[i - 2] = at_first(low, d2[i - 1], d2[i - 2])
                    if i - 1 in emit_detail:
                        emit(level, outs[level], i - 1, d2[i - 1] * (KAPPA / SQRT_TWO))
                    if i - 1 in emit_approx:
                        s2 = s1[i - 1] + DELTA * (d2[i - 2] + d2[i - 1])
                        approx = s2 * (SQRT_TWO / KAPPA)
                        if final:
                            emit(LEVELS, outs[LEVELS], i - 1, approx)
                        else:
                            inputs[level + 1][f, i - 1, at] = approx
            for kind, total in sums.items():
                acc[f, kind] += total

    lane = lax.broadcasted_iota(jnp.int32, (1, 128), 1)

    def reduced(f, row, kinds):
        for b in kinds:
            total = jnp.sum(jnp.sum(acc[f, b], axis=0, keepdims=True), axis=1, keepdims=True)
            row = jnp.where(lane == b, total, row)
        return row

    def analyse(head):
        slow_peer, fast_peer = (gz - 1, gz + 1) if head else (gz + 1, gz - 1)
        has_slow = gz > 0 if head else gz < gz_count - 1
        slow_copy = lambda level, c: copy_of(
            slow_send, slow_recv, slow_send_sem, slow_recv_sem, level, c, slow_peer
        )
        fast_copy = lambda level, c: copy_of(
            fast_send, fast_recv, fast_send_sem, fast_recv_sem, level, c, fast_peer
        )
        touched = HEAD_TOUCHED if head else TAIL_TOUCHED
        far = (TRAIL_TAIL if head else TRAIL_HEAD)[1:] + ((3,) if head else (4,))
        top = LEVELS - 2

        def ends(slow, fast):
            return (slow, fast) if head else (fast, slow)

        def slow_start(level, c):
            @pl.when(has_slow)
            def _():
                slow_copy(level, c).start()

        def bulk(level, c):
            half = inputs[level].shape[1] // 2
            details, _ = touched[level]
            keep = range(max(details, 1), half - 2) if head else range(1, half - max(details, 2))
            lift(level, c, 0, half - 1, None, None, keep, range(2, half - 2))
            rim(level, c, head, "local", 0, 2)

        def rim(level, c, low_end, kind, details, approx):
            half = inputs[level].shape[1] // 2
            if low_end:
                lift(level, c, 0, approx + 1, kind, None, range(details), range(approx))
            else:
                begin = half - approx - 2
                span = lambda n: range(half - n, half)
                lift(level, c, begin, half, None, kind, span(details), span(approx))

        def fast_rim(level, c):
            if level < top:
                rim(level, c, not head, "fast", 2 if head else 1, 2)
            else:
                half = inputs[level].shape[1] // 2
                lift(level, c, 0, half, *ends("local", "fast"), range(0), range(half))

        def reach_back(level, c):
            count = (TRAIL_TAIL if head else TRAIL_HEAD)[level]
            for f, at, to in tiles(c):
                states = states_of(level, f, at, head)
                if head:
                    entry = lambda j: trail[c, -1 - j, to] if -count <= j < 0 else None
                else:
                    entry = lambda j: trail[c, j, to] if 0 <= j < count else None
                added = echo(entry, states, not head)
                keep = far[level]
                for n in range(keep):
                    trail[c, n, to] = added[-1 - n if head else n]
                after = lambda j: added[j] if (-1 - j if head else j) < keep else None
                one, two = (tail_states if head else head_states)(after)
                bias[c, 0, to] = one
                bias[c, 1, to] = two

        def settle(level, c):
            if level < top:
                rim(level, c, head, "slow", *touched[level])
            else:
                half = inputs[level].shape[1] // 2
                lift(level, c, 0, half, *ends("slow", "fast"), range(half), range(half))

        edge_copy(0).wait()
        edge_copy(1).wait()

        @pl.loop(0, chunks)
        def _(c):
            put_states(slow_send, 0, c, head)
            put_states(fast_send, 0, c, not head)

        limit_copy.wait()
        pl.semaphore_wait(barrier, beside(1) + xy_count - 1)

        @pl.loop(0, chunks)
        def _(c):
            slow_start(0, c)
            fast_copy(0, c).start()

        ready_signal(0)

        @pl.loop(0, chunks)
        def _(c):
            body_copy(c).wait()
            bulk(0, c)
            put_states(slow_send, 1, c, head)
            slow_start(1, c)

        for level in range(top + 1):

            @pl.loop(0, chunks)
            def _(c):
                fast_copy(level, c).wait_recv()
                fast_rim(level, c)
                if level < top:
                    put_states(fast_send, level + 1, c, not head)
                    fast_copy(level + 1, c).start()
                if level + 1 < top:
                    bulk(level + 1, c)
                if level + 2 <= top:
                    put_states(slow_send, level + 2, c, head)
                    slow_start(level + 2, c)
                if level == top:
                    put_states(slow_send, top + 1, c, head)
                    slow_start(top + 1, c)

        for level in range(top + 1):
            ready_wait(level)
            ready_signal(level + 1)

            @pl.loop(0, chunks)
            def _(c):
                @pl.when(has_slow)
                def _():
                    slow_copy(level, c).wait_recv()

                settle(level, c)
                reach_back(level, c)
                if level == top:
                    put_states(fast_send, top + 1, c, not head)
                    fast_copy(top + 1, c).start()

        for stage in range(top + 1, stages):
            ready_wait(stage)
            ready_signal(stage + 1)

        zero = jnp.zeros((1, 128), jnp.float32)
        for f in range(field_count):
            e_send_buf[pl.ds(f, 1), :] = reduced(f, zero, range(top + 1))

        @pl.loop(0, chunks)
        def _(c):
            fast_copy(top + 1, c).wait_recv()

            @pl.when(has_slow)
            def _():
                slow_copy(top + 1, c).wait_recv()

            lift(top + 1, c, 0, 2, *ends("slow", "fast"), range(2), range(2))

    @pl.when(even)
    def _():
        analyse(True)

    @pl.when(jnp.logical_not(even))
    def _():
        analyse(False)

    for f in range(field_count):
        row = e_send_buf[pl.ds(f, 1), :]
        e_send_buf[pl.ds(f, 1), :] = reduced(f, row, range(LEVELS - 1, LEVELS + 1))

    def energy_copy(peer):
        return pltpu.make_async_remote_copy(
            src_ref=e_send_buf,
            dst_ref=e_recv_buf.at[me],
            send_sem=e_send_sem,
            recv_sem=e_recv_sem,
            device_id=peer,
            device_id_type=MESH,
        )

    for_peers(lambda peer: energy_copy(peer).start())

    e_recv_buf[me] = e_send_buf[...]

    slow_any, fast_any = jnp.where(even, gz - 1, gz + 1), jnp.where(even, gz + 1, gz - 1)

    @pl.loop(0, chunks)
    def _(c):
        for level in range(LEVELS):
            copy_of(
                fast_send, fast_recv, fast_send_sem, fast_recv_sem, level, c, fast_any
            ).wait_send()

            @pl.when(jnp.logical_and(slow_any >= 0, slow_any < gz_count))
            def _():
                copy_of(
                    slow_send, slow_recv, slow_send_sem, slow_recv_sem, level, c, slow_any
                ).wait_send()

    others = e_recv_buf.at[pl.ds(0, devices - 1)]
    pltpu.make_async_copy(others, others, e_recv_sem).wait()

    totals = jnp.sum(e_recv_buf[...], axis=0)
    cells = jnp.ones((1, 128), jnp.float32)
    for b in range(LEVELS + 1):
        shape = outs[b].shape
        cells = jnp.where(lane == b, float(shape[1] * shape[2] * shape[3] * devices), cells)
    energy_ref[...] = (totals / cells)[:, : LEVELS + 1]

    pltpu.make_async_copy(others, others, e_send_sem).wait()


def write_out(*refs):
    count = (len(refs) - 1) // 2
    sources, targets, sems = refs[:count], refs[count : 2 * count], refs[-1]
    copies = [
        pltpu.make_async_copy(source, target, sems.at[k])
        for k, (source, target) in enumerate(zip(sources, targets))
    ]
    for copy in copies:
        copy.start()
    for copy in copies:
        copy.wait()


def solution(mesh):
    gz_count, xy_count = mesh.shape["gz"], mesh.shape["xy"]
    devices = gz_count * xy_count

    def local(fields, threshold):
        field_count, layers, width, depth = fields.shape
        chunks = field_count * (width // ROWS)
        assert gz_count % 2 == 0 and layers >> (LEVELS - 2) == 8
        f32 = jnp.float32
        halves = [layers >> (level + 1) for level in range(LEVELS)]
        band_layers = halves + halves[-1:]
        vmem = pl.BlockSpec(memory_space=pltpu.VMEM)
        shapes = tuple(
            jax.ShapeDtypeStruct((field_count, n, width, depth), f32) for n in band_layers
        ) + (jax.ShapeDtypeStruct((field_count, LEVELS + 1), f32),)
        results = pl.pallas_call(
            functools.partial(kernel, gz_count, xy_count),
            out_shape=tuple(pltpu.VMEM(shape.shape, shape.dtype) for shape in shapes),
            in_specs=[
                pl.BlockSpec(memory_space=pltpu.HBM),
                pl.BlockSpec(memory_space=pltpu.HBM),
            ],
            out_specs=(vmem,) * (LEVELS + 2),
            scratch_shapes=[
                pltpu.VMEM((field_count, n, width, depth), f32) for n in [layers] + halves[:-1]
            ]
            + [
                pltpu.VMEM((LEVELS, chunks, 2, ROWS, depth), f32),
                pltpu.VMEM((LEVELS, chunks, 2, ROWS, depth), f32),
                pltpu.VMEM((LEVELS, chunks, 2, ROWS, depth), f32),
                pltpu.VMEM((LEVELS, chunks, 2, ROWS, depth), f32),
                pltpu.VMEM((chunks, 2, ROWS, depth), f32),
                pltpu.VMEM((chunks, 4, ROWS, depth), f32),
                pltpu.VMEM((field_count, LEVELS + 1, SUB, depth), f32),
                pltpu.VMEM((field_count, 128), f32),
                pltpu.VMEM((devices, field_count, 128), f32),
                pltpu.SMEM((field_count,), f32),
                pltpu.SemaphoreType.DMA((chunks,)),
                pltpu.SemaphoreType.DMA((2,)),
                pltpu.SemaphoreType.DMA((LEVELS, chunks)),
                pltpu.SemaphoreType.DMA((LEVELS, chunks)),
                pltpu.SemaphoreType.DMA((LEVELS, chunks)),
                pltpu.SemaphoreType.DMA((LEVELS, chunks)),
                pltpu.SemaphoreType.DMA,
                pltpu.SemaphoreType.DMA,
                pltpu.SemaphoreType.DMA,
                pltpu.SemaphoreType.REGULAR(((gz_count - 1).bit_length(),)),
            ],
            compiler_params=pltpu.CompilerParams(
                collective_id=0,
                has_side_effects=True,
                vmem_limit_bytes=32 * 1024 * 1024,
            ),
        )(
            pltpu.with_memory_space_constraint(threshold, pltpu.HBM),
            pltpu.with_memory_space_constraint(fields, pltpu.HBM),
        )
        return pl.pallas_call(
            write_out,
            out_shape=shapes,
            in_specs=[vmem] * (LEVELS + 2),
            out_specs=(pl.BlockSpec(memory_space=pltpu.HBM),) * (LEVELS + 2),
            scratch_shapes=[pltpu.SemaphoreType.DMA((LEVELS + 2,))],
            compiler_params=pltpu.CompilerParams(vmem_limit_bytes=4 * 1024 * 1024),
        )(*(pltpu.with_memory_space_constraint(result, pltpu.VMEM) for result in results))

    banded = P(None, "gz", "xy", None)
    return jax.shard_map(
        local,
        mesh=mesh,
        in_specs=(banded, P()),
        out_specs=(banded,) * (LEVELS + 1) + (P(),),
        check_vma=False,
    )
```

```python
import functools

import jax
import jax.numpy as jnp
from jax import lax
from jax.experimental import pallas as pl
from jax.experimental.pallas import tpu as pltpu
from jax.sharding import PartitionSpec as P

ALPHA = -1.586134342059924
BETA = -0.052980118572961
GAMMA = 0.882911075530934
DELTA = 0.443506852043971
KAPPA = 1.230174104914001
SQRT_TWO = 1.4142135623730951
LEVELS = 5
MESH = pl.DeviceIdType.MESH
SUB = 8
ROWS = 16
AHEAD = 2


def plus(*terms):
    terms = [term for term in terms if term is not None]
    return functools.reduce(lambda x, y: x + y, terms) if terms else None


def times(factor, value):
    return None if value is None else factor * value


def head_states(entry):
    s_head, d_head, s_after = (entry(j) for j in range(3))
    d_lifted = plus(d_head, times(ALPHA, plus(s_head, s_after)))
    return s_head, plus(s_head, times(BETA, d_lifted))


def tail_states(entry):
    s_prev, d_prev, s_tail, d_tail = (entry(j) for j in range(-4, 0))
    d_lifted = plus(d_prev, times(ALPHA, plus(s_prev, s_tail)))
    return plus(d_tail, times(ALPHA, s_tail)), plus(s_tail, times(BETA, d_lifted))


def echo(entry, states, head):
    reach = range(-1, 4) if head else range(-4, 1)
    inside = (lambda j: j >= 0) if head else (lambda j: j < 0)
    s = {j: entry(2 * j) for j in reach if inside(j)}
    d = {j: entry(2 * j + 1) for j in reach if inside(j)}
    if not head:
        s[0] = states[0]
    d1, s1, d2, s2 = {}, {}, {}, {}
    for j in reach:
        if inside(j):
            d1[j] = plus(d.get(j), times(ALPHA, plus(s.get(j), s.get(j + 1))))
    if head:
        d1[-1] = plus(states[0], times(ALPHA, s[0]))
    for j in reach:
        if inside(j):
            s1[j] = plus(s.get(j), times(BETA, plus(d1.get(j - 1), d1.get(j))))
    beyond = -1 if head else 0
    s1[beyond] = plus(states[1], times(BETA, d1[-1]))
    for j in range(-1, 4) if head else range(-4, 0):
        d2[j] = plus(d1.get(j), times(GAMMA, plus(s1.get(j), s1.get(j + 1))))
    for j in reach:
        if inside(j):
            s2[j] = plus(s1.get(j), times(DELTA, plus(d2.get(j - 1), d2.get(j))))
    return {j: times(SQRT_TWO / KAPPA, value) for j, value in s2.items() if value is not None}


HEAD_TOUCHED = ((1, 2), (2, 3), (3, 4))
TAIL_TOUCHED = ((2, 2), (3, 3), (3, 3))
TRAIL_HEAD = (0, 2, 3, 4)
TRAIL_TAIL = (0, 2, 3, 3)


def kernel(
    gz_count,
    xy_count,
    relay,
    threshold_hbm,
    fields_ref,
    *refs,
):
    outs = refs[: LEVELS + 1]
    energy_ref = refs[LEVELS + 1]
    inputs = refs[LEVELS + 2 : 2 * LEVELS + 2]
    (
        slow_send,
        slow_recv,
        fast_send,
        fast_recv,
        relay_buf,
        bias,
        trail,
        acc,
        e_send_buf,
        e_recv_buf,
    ) = refs[2 * LEVELS + 2 : 2 * LEVELS + 12]
    (
        threshold_ref,
        in_sem,
        edge_sem,
        slow_send_sem,
        slow_recv_sem,
        fast_send_sem,
        fast_recv_sem,
        relay_send_sem,
        relay_recv_sem,
        e_send_sem,
        e_recv_sem,
        limit_sem,
        ready_sem,
    ) = refs[2 * LEVELS + 12 :]
    field_count, layers, width, _ = fields_ref.shape
    per_field = width // ROWS
    chunks = field_count * per_field
    devices = gz_count * xy_count
    stages = (gz_count - 1).bit_length()

    gz = lax.axis_index("gz")
    xy = lax.axis_index("xy")
    me = gz * xy_count + xy
    first = gz == 0
    last = gz == gz_count - 1
    even = lax.rem(gz, 2) == 0

    def wrapped(value, step, count):
        moved = value + step
        return jnp.where(moved >= count, moved - count, moved)

    def for_peers(act):
        for across in range(1, xy_count):
            act((gz, wrapped(xy, across, xy_count)))

        @pl.loop(1, gz_count)
        def _(along):
            for across in range(xy_count):
                act((wrapped(gz, along, gz_count), wrapped(xy, across, xy_count)))

    def for_both(step, act):
        @pl.when(gz >= step)
        def _():
            act(gz - step)

        @pl.when(gz < gz_count - step)
        def _():
            act(gz + step)

    def beside(step):
        return (gz >= step).astype(jnp.int32) + (gz < gz_count - step).astype(jnp.int32)

    barrier = pltpu.get_barrier_semaphore()

    def signal(sem, peer):
        pl.semaphore_signal(sem, inc=1, device_id=peer, device_id_type=MESH)

    for_both(1, lambda peer: signal(barrier, (peer, xy)))
    corner = jnp.logical_or(lax.rem(gz, 4) == 0, lax.rem(gz, 4) == 3)
    partner = jnp.where(even, gz + 3, gz - 3)
    if relay:

        @pl.when(corner)
        def _():
            signal(barrier, (partner, xy))

    for across in range(1, xy_count):
        signal(barrier, (gz, wrapped(xy, across, xy_count)))

    def ready_signal(k):
        if k < stages:
            for_both(1 << k, lambda peer: signal(ready_sem.at[k], (peer, xy)))

    def ready_wait(k):
        if k < stages:
            pl.semaphore_wait(ready_sem.at[k], beside(1 << k))

    def place(c):
        return c // per_field, pl.multiple_of(lax.rem(c, per_field) * ROWS, ROWS)

    def edge_copy(side):
        part = pl.ds(0 if side == 0 else layers - 4, 4)
        return pltpu.make_async_copy(
            fields_ref.at[:, part], inputs[0].at[:, part], edge_sem.at[side]
        )

    def body_copy(c):
        f, row = place(c)
        where = (f, pl.ds(4, layers - 8), pl.ds(row, ROWS))
        return pltpu.make_async_copy(
            fields_ref.at[where], inputs[0].at[where], in_sem.at[c]
        )

    edge_copy(0).start()
    edge_copy(1).start()
    limit_copy = pltpu.make_async_copy(threshold_hbm, threshold_ref, limit_sem)
    limit_copy.start()

    @pl.loop(0, chunks)
    def _(c):
        body_copy(c).start()

    acc[...] = jnp.zeros_like(acc)

    def tiles(c):
        f, row = place(c)
        for t in range(ROWS // SUB):
            yield f, pl.ds(pl.multiple_of(row + t * SUB, SUB), SUB), pl.ds(t * SUB, SUB)

    def states_of(level, f, at, head):
        source = inputs[level]
        count = source.shape[1]
        make = head_states if head else tail_states
        return make(lambda j: source[f, j if j >= 0 else count + j, at])

    def put_states(buf, level, c, head):
        for f, at, to in tiles(c):
            one, two = states_of(level, f, at, head)
            buf[level, c, 0, to] = one
            buf[level, c, 1, to] = two

    units = LEVELS * chunks
    rows_between = gz_count // 4 - 1

    def by_relay(level, c, up, boundary):
        if up:
            share = (rows_between - boundary) * units // (rows_between + 1)
        else:
            share = (boundary + 1) * (boundary + 1) * units // (rows_between + 1) ** 2
        unit = level * chunks + c
        return (unit + 1) * share // units > unit * share // units

    def copy_of(send, recv, send_sem, recv_sem, level, c, peer):
        return pltpu.make_async_remote_copy(
            src_ref=send.at[level, c],
            dst_ref=recv.at[level, c],
            send_sem=send_sem.at[level, c],
            recv_sem=recv_sem.at[level, c],
            device_id={"gz": peer},
            device_id_type=MESH,
        )

    def lift(level, c, begin, end, low, high, emit_detail, emit_approx):
        source = inputs[level]
        half = source.shape[1] // 2
        final = level == LEVELS - 1
        limit = threshold_ref[c // per_field]

        def shrink(band):
            return band - jnp.minimum(jnp.maximum(band, -limit), limit)

        for f, at, to in tiles(c):
            evens = lambda i: source[f, 2 * i, at]
            odds = lambda i: source[f, 2 * i + 1, at]
            d1, s1, d2, sums = {}, {}, {}, {}

            def incoming(kind, which):
                if kind == "fast":
                    return fast_recv[level, c, which, to]
                if kind == "slow":
                    value = slow_recv[level, c, which, to]
                    return value + bias[c, which, to] if level else value
                return None

            def at_first(kind, mirrored, outer):
                return outer if kind == "fast" else jnp.where(first, mirrored, outer)

            def at_last(kind, mirrored, outer):
                outer = jnp.zeros_like(mirrored) if outer is None else outer
                return outer if kind == "fast" else jnp.where(last, mirrored, outer)

            def emit(kind, ref, i, value):
                band = shrink(value)
                ref[f, i, at] = band
                square = band * band
                sums[kind] = sums[kind] + square if kind in sums else square

            s = evens(begin)
            for i in range(begin, end + 1):
                if i < end:
                    if i + 1 < half:
                        s_next = evens(i + 1)
                    else:
                        s_next = at_last(high, s, incoming(high, 0))
                    d1[i] = odds(i) + ALPHA * (s + s_next)
                    if i == begin and low:
                        d1[i - 1] = at_first(low, d1[i], plus(incoming(low, 0), ALPHA * s))
                    if i - 1 in d1:
                        s1[i] = s + BETA * (d1[i - 1] + d1[i])
                    if i == begin and low:
                        s1[i - 1] = plus(incoming(low, 1), BETA * d1[i - 1])
                        d2[i - 1] = d1[i - 1] + GAMMA * (s1[i - 1] + s1[i])
                    s = s_next
                elif high:
                    s1[i] = at_last(high, s1[i - 1], plus(incoming(high, 1), BETA * d1[i - 1]))
                if i > begin and i - 1 in s1 and i in s1:
                    d2[i - 1] = d1[i - 1] + GAMMA * (s1[i - 1] + s1[i])
                    if i - 1 == begin and low:
                        d2[i - 2] = at_first(low, d2[i - 1], d2[i - 2])
                    if i - 1 in emit_detail:
                        emit(level, outs[level], i - 1, d2[i - 1] * (KAPPA / SQRT_TWO))
                    if i - 1 in emit_approx:
                        s2 = s1[i - 1] + DELTA * (d2[i - 2] + d2[i - 1])
                        approx = s2 * (SQRT_TWO / KAPPA)
                        if final:
                            emit(LEVELS, outs[LEVELS], i - 1, approx)
                        else:
                            inputs[level + 1][f, i - 1, at] = approx
            for kind, total in sums.items():
                acc[f, kind] += total

    lane = lax.broadcasted_iota(jnp.int32, (1, 128), 1)

    def reduced(f, row, kinds):
        for b in kinds:
            total = jnp.sum(jnp.sum(acc[f, b], axis=0, keepdims=True), axis=1, keepdims=True)
            row = jnp.where(lane == b, total, row)
        return row

    def analyse(head):
        slow_peer, fast_peer = (gz - 1, gz + 1) if head else (gz + 1, gz - 1)
        has_slow = gz > 0 if head else gz < gz_count - 1
        slow_copy = lambda level, c: copy_of(
            slow_send, slow_recv, slow_send_sem, slow_recv_sem, level, c, slow_peer
        )
        fast_copy = lambda level, c: copy_of(
            fast_send, fast_recv, fast_send_sem, fast_recv_sem, level, c, fast_peer
        )
        touched = HEAD_TOUCHED if head else TAIL_TOUCHED
        far = (TRAIL_TAIL if head else TRAIL_HEAD)[1:] + ((3,) if head else (4,))
        top = LEVELS - 2

        def ends(slow, fast):
            return (slow, fast) if head else (fast, slow)

        relay_copy = lambda level, c: copy_of(
            slow_send, relay_buf, slow_send_sem, relay_recv_sem, level, c, partner
        )
        onward_copy = lambda level, c: copy_of(
            relay_buf, slow_recv, relay_send_sem, slow_recv_sem, level, c, gz + 4 if head else gz - 4
        )
        turn = jnp.logical_and(corner, has_slow)
        passes = jnp.logical_and(corner, gz < gz_count - 4 if head else gz >= 4)
        row = gz // 4

        def slow_start(level, c):
            if not relay:

                @pl.when(has_slow)
                def _():
                    slow_copy(level, c).start()

                return
            turned = jnp.logical_and(turn, by_relay(level, c, not head, row - 1 if head else row))

            @pl.when(turned)
            def _():
                relay_copy(level, c).start()

            @pl.when(jnp.logical_and(has_slow, jnp.logical_not(turned)))
            def _():
                slow_copy(level, c).start()

        def pass_on(level, c, act):
            if relay:
                passed = by_relay(level, c, head, row if head else row - 1)

                @pl.when(jnp.logical_and(passes, passed))
                def _():
                    act(level, c)

        def receive_and_send(level, c):
            relay_copy(level, c).wait_recv()
            onward_copy(level, c).start()

        def bulk(level, c):
            half = inputs[level].shape[1] // 2
            details, _ = touched[level]
            keep = range(max(details, 1), half - 2) if head else range(1, half - max(details, 2))
            lift(level, c, 0, half - 1, None, None, keep, range(2, half - 2))
            rim(level, c, head, "local", 0, 2)

        def rim(level, c, low_end, kind, details, approx):
            half = inputs[level].shape[1] // 2
            if low_end:
                lift(level, c, 0, approx + 1, kind, None, range(details), range(approx))
            else:
                begin = half - approx - 2
                span = lambda n: range(half - n, half)
                lift(level, c, begin, half, None, kind, span(details), span(approx))

        def fast_rim(level, c):
            if level < top:
                rim(level, c, not head, "fast", 2 if head else 1, 2)
            else:
                half = inputs[level].shape[1] // 2
                lift(level, c, 0, half, *ends("local", "fast"), range(0), range(half))

        def reach_back(level, c):
            count = (TRAIL_TAIL if head else TRAIL_HEAD)[level]
            for f, at, to in tiles(c):
                states = states_of(level, f, at, head)
                if head:
                    entry = lambda j: trail[c, -1 - j, to] if -count <= j < 0 else None
                else:
                    entry = lambda j: trail[c, j, to] if 0 <= j < count else None
                added = echo(entry, states, not head)
                keep = far[level]
                for n in range(keep):
                    trail[c, n, to] = added[-1 - n if head else n]
                after = lambda j: added[j] if (-1 - j if head else j) < keep else None
                one, two = (tail_states if head else head_states)(after)
                bias[c, 0, to] = one
                bias[c, 1, to] = two

        def settle(level, c):
            if level < top:
                rim(level, c, head, "slow", *touched[level])
            else:
                half = inputs[level].shape[1] // 2
                lift(level, c, 0, half, *ends("slow", "fast"), range(half), range(half))

        edge_copy(0).wait()
        edge_copy(1).wait()

        @pl.loop(0, chunks)
        def _(c):
            put_states(slow_send, 0, c, head)
            put_states(fast_send, 0, c, not head)

        limit_copy.wait()
        greeted = corner.astype(jnp.int32) if relay else 0
        pl.semaphore_wait(barrier, beside(1) + greeted + xy_count - 1)

        @pl.loop(0, chunks)
        def _(c):
            slow_start(0, c)
            fast_copy(0, c).start()

        ready_signal(0)

        @pl.loop(0, chunks)
        def _(c):
            body_copy(c).wait()
            bulk(0, c)
            put_states(slow_send, 1, c, head)
            slow_start(1, c)

        ready_wait(0)
        ready_signal(1)

        for level in range(top + 1):

            @pl.loop(0, chunks)
            def _(c):
                fast_copy(level, c).wait_recv()
                fast_rim(level, c)
                if level < top:
                    put_states(fast_send, level + 1, c, not head)
                    fast_copy(level + 1, c).start()
                if level + 1 < top:
                    bulk(level + 1, c)
                if level + 2 <= top:
                    put_states(slow_send, level + 2, c, head)
                    slow_start(level + 2, c)
                if level == top:
                    put_states(slow_send, top + 1, c, head)
                    slow_start(top + 1, c)

        ready_wait(1)
        ready_signal(2)
        if relay:

            @pl.loop(0, chunks)
            def _(c):
                for level in range(AHEAD):
                    pass_on(level, c, receive_and_send)

        for level in range(top + 1):
            if level:
                ready_wait(level + 1)
                ready_signal(level + 2)

            @pl.loop(0, chunks)
            def _(c):
                if level + AHEAD < LEVELS:
                    pass_on(level + AHEAD, c, receive_and_send)

                @pl.when(has_slow)
                def _():
                    slow_copy(level, c).wait_recv()

                settle(level, c)
                reach_back(level, c)
                if level == top:
                    put_states(fast_send, top + 1, c, not head)
                    fast_copy(top + 1, c).start()

        for stage in range(top + 2, stages):
            ready_wait(stage)
            ready_signal(stage + 1)

        zero = jnp.zeros((1, 128), jnp.float32)
        for f in range(field_count):
            e_send_buf[pl.ds(f, 1), :] = reduced(f, zero, range(top + 1))

        @pl.loop(0, chunks)
        def _(c):
            fast_copy(top + 1, c).wait_recv()

            @pl.when(has_slow)
            def _():
                slow_copy(top + 1, c).wait_recv()

            lift(top + 1, c, 0, 2, *ends("slow", "fast"), range(2), range(2))

        return lambda level, c: pass_on(level, c, lambda *at: onward_copy(*at).wait_send())

    def energy_copy(peer):
        return pltpu.make_async_remote_copy(
            src_ref=e_send_buf,
            dst_ref=e_recv_buf.at[me],
            send_sem=e_send_sem,
            recv_sem=e_recv_sem,
            device_id=peer,
            device_id_type=MESH,
        )

    def send_energies():
        for f in range(field_count):
            row = e_send_buf[pl.ds(f, 1), :]
            e_send_buf[pl.ds(f, 1), :] = reduced(f, row, range(LEVELS - 1, LEVELS + 1))
        for_peers(lambda peer: energy_copy(peer).start())

    def whole(head):
        finish = analyse(head)
        send_energies()
        if relay:

            @pl.loop(0, chunks)
            def _(c):
                for level in range(LEVELS):
                    finish(level, c)

    @pl.when(even)
    def _():
        whole(True)

    @pl.when(jnp.logical_not(even))
    def _():
        whole(False)

    e_recv_buf[me] = e_send_buf[...]

    slow_any, fast_any = jnp.where(even, gz - 1, gz + 1), jnp.where(even, gz + 1, gz - 1)

    @pl.loop(0, chunks)
    def _(c):
        for level in range(LEVELS):
            copy_of(
                fast_send, fast_recv, fast_send_sem, fast_recv_sem, level, c, fast_any
            ).wait_send()

            @pl.when(jnp.logical_and(slow_any >= 0, slow_any < gz_count))
            def _():
                copy_of(
                    slow_send, slow_recv, slow_send_sem, slow_recv_sem, level, c, slow_any
                ).wait_send()

    others = e_recv_buf.at[pl.ds(0, devices - 1)]
    pltpu.make_async_copy(others, others, e_recv_sem).wait()

    totals = jnp.sum(e_recv_buf[...], axis=0)
    cells = jnp.ones((1, 128), jnp.float32)
    for b in range(LEVELS + 1):
        shape = outs[b].shape
        cells = jnp.where(lane == b, float(shape[1] * shape[2] * shape[3] * devices), cells)
    energy_ref[...] = (totals / cells)[:, : LEVELS + 1]

    pltpu.make_async_copy(others, others, e_send_sem).wait()


def write_out(*refs):
    count = (len(refs) - 1) // 2
    sources, targets, sems = refs[:count], refs[count : 2 * count], refs[-1]
    copies = [
        pltpu.make_async_copy(source, target, sems.at[k])
        for k, (source, target) in enumerate(zip(sources, targets))
    ]
    for copy in copies:
        copy.start()
    for copy in copies:
        copy.wait()


def zigzag(mesh):
    line = [getattr(device, "coords", None) for device in mesh.devices[:, 0]]
    if len(line) % 4 or None in line:
        return False
    apart = lambda a, b: sum(abs(p - q) for p, q in zip(line[a], line[b]))
    return all(
        (apart(g, g + 1), apart(g, g - 3), apart(g - 3, g + 1), apart(g + 1, g + 4), apart(g + 4, g))
        == (2, 1, 1, 1, 1)
        for g in range(3, len(line) - 1, 4)
    )


def solution(mesh):
    relay = zigzag(mesh)
    gz_count, xy_count = mesh.shape["gz"], mesh.shape["xy"]
    devices = gz_count * xy_count

    def local(fields, threshold):
        field_count, layers, width, depth = fields.shape
        chunks = field_count * (width // ROWS)
        assert gz_count % 2 == 0 and layers >> (LEVELS - 2) == 8
        f32 = jnp.float32
        halves = [layers >> (level + 1) for level in range(LEVELS)]
        band_layers = halves + halves[-1:]
        vmem = pl.BlockSpec(memory_space=pltpu.VMEM)
        shapes = tuple(
            jax.ShapeDtypeStruct((field_count, n, width, depth), f32) for n in band_layers
        ) + (jax.ShapeDtypeStruct((field_count, LEVELS + 1), f32),)
        results = pl.pallas_call(
            functools.partial(kernel, gz_count, xy_count, relay),
            out_shape=tuple(pltpu.VMEM(shape.shape, shape.dtype) for shape in shapes),
            in_specs=[
                pl.BlockSpec(memory_space=pltpu.HBM),
                pl.BlockSpec(memory_space=pltpu.HBM),
            ],
            out_specs=(vmem,) * (LEVELS + 2),
            scratch_shapes=[
                pltpu.VMEM((field_count, n, width, depth), f32) for n in [layers] + halves[:-1]
            ]
            + [
                pltpu.VMEM((LEVELS, chunks, 2, ROWS, depth), f32),
                pltpu.VMEM((LEVELS, chunks, 2, ROWS, depth), f32),
                pltpu.VMEM((LEVELS, chunks, 2, ROWS, depth), f32),
                pltpu.VMEM((LEVELS, chunks, 2, ROWS, depth), f32),
                pltpu.VMEM((LEVELS, chunks, 2, ROWS, depth), f32),
                pltpu.VMEM((chunks, 2, ROWS, depth), f32),
                pltpu.VMEM((chunks, 4, ROWS, depth), f32),
                pltpu.VMEM((field_count, LEVELS + 1, SUB, depth), f32),
                pltpu.VMEM((field_count, 128), f32),
                pltpu.VMEM((devices, field_count, 128), f32),
                pltpu.SMEM((field_count,), f32),
                pltpu.SemaphoreType.DMA((chunks,)),
                pltpu.SemaphoreType.DMA((2,)),
                pltpu.SemaphoreType.DMA((LEVELS, chunks)),
                pltpu.SemaphoreType.DMA((LEVELS, chunks)),
                pltpu.SemaphoreType.DMA((LEVELS, chunks)),
                pltpu.SemaphoreType.DMA((LEVELS, chunks)),
                pltpu.SemaphoreType.DMA((LEVELS, chunks)),
                pltpu.SemaphoreType.DMA((LEVELS, chunks)),
                pltpu.SemaphoreType.DMA,
                pltpu.SemaphoreType.DMA,
                pltpu.SemaphoreType.DMA,
                pltpu.SemaphoreType.REGULAR(((gz_count - 1).bit_length(),)),
            ],
            compiler_params=pltpu.CompilerParams(
                collective_id=0,
                has_side_effects=True,
                vmem_limit_bytes=32 * 1024 * 1024,
            ),
        )(
            pltpu.with_memory_space_constraint(threshold, pltpu.HBM),
            pltpu.with_memory_space_constraint(fields, pltpu.HBM),
        )
        return pl.pallas_call(
            write_out,
            out_shape=shapes,
            in_specs=[vmem] * (LEVELS + 2),
            out_specs=(pl.BlockSpec(memory_space=pltpu.HBM),) * (LEVELS + 2),
            scratch_shapes=[pltpu.SemaphoreType.DMA((LEVELS + 2,))],
            compiler_params=pltpu.CompilerParams(vmem_limit_bytes=4 * 1024 * 1024),
        )(*(pltpu.with_memory_space_constraint(result, pltpu.VMEM) for result in results))

    banded = P(None, "gz", "xy", None)
    return jax.shard_map(
        local,
        mesh=mesh,
        in_specs=(banded, P()),
        out_specs=(banded,) * (LEVELS + 1) + (P(),),
        check_vma=False,
    )
```

```python
import functools

import jax
import jax.numpy as jnp
from jax import lax
from jax.experimental import pallas as pl
from jax.experimental.pallas import tpu as pltpu
from jax.sharding import PartitionSpec as P

ALPHA = -1.586134342059924
BETA = -0.052980118572961
GAMMA = 0.882911075530934
DELTA = 0.443506852043971
KAPPA = 1.230174104914001
SQRT_TWO = 1.4142135623730951
LEVELS = 5
MESH = pl.DeviceIdType.MESH
SUB = 8
ROWS = 16
AHEAD = 2


def plus(*terms):
    terms = [term for term in terms if term is not None]
    return functools.reduce(lambda x, y: x + y, terms) if terms else None


def times(factor, value):
    return None if value is None else factor * value


def head_states(entry):
    s_head, d_head, s_after = (entry(j) for j in range(3))
    d_lifted = plus(d_head, times(ALPHA, plus(s_head, s_after)))
    return s_head, plus(s_head, times(BETA, d_lifted))


def tail_states(entry):
    s_prev, d_prev, s_tail, d_tail = (entry(j) for j in range(-4, 0))
    d_lifted = plus(d_prev, times(ALPHA, plus(s_prev, s_tail)))
    return plus(d_tail, times(ALPHA, s_tail)), plus(s_tail, times(BETA, d_lifted))


def echo(entry, states, head):
    reach = range(-1, 4) if head else range(-4, 1)
    inside = (lambda j: j >= 0) if head else (lambda j: j < 0)
    s = {j: entry(2 * j) for j in reach if inside(j)}
    d = {j: entry(2 * j + 1) for j in reach if inside(j)}
    if not head:
        s[0] = states[0]
    d1, s1, d2, s2 = {}, {}, {}, {}
    for j in reach:
        if inside(j):
            d1[j] = plus(d.get(j), times(ALPHA, plus(s.get(j), s.get(j + 1))))
    if head:
        d1[-1] = plus(states[0], times(ALPHA, s[0]))
    for j in reach:
        if inside(j):
            s1[j] = plus(s.get(j), times(BETA, plus(d1.get(j - 1), d1.get(j))))
    beyond = -1 if head else 0
    s1[beyond] = plus(states[1], times(BETA, d1[-1]))
    for j in range(-1, 4) if head else range(-4, 0):
        d2[j] = plus(d1.get(j), times(GAMMA, plus(s1.get(j), s1.get(j + 1))))
    for j in reach:
        if inside(j):
            s2[j] = plus(s1.get(j), times(DELTA, plus(d2.get(j - 1), d2.get(j))))
    return {j: times(SQRT_TWO / KAPPA, value) for j, value in s2.items() if value is not None}


HEAD_TOUCHED = ((1, 2), (2, 3), (3, 4))
TAIL_TOUCHED = ((2, 2), (3, 3), (3, 3))
TRAIL_HEAD = (0, 2, 3, 4)
TRAIL_TAIL = (0, 2, 3, 3)


def kernel(
    gz_count,
    xy_count,
    relay,
    threshold_hbm,
    fields_ref,
    *refs,
):
    outs = refs[: LEVELS + 1]
    energy_ref = refs[LEVELS + 1]
    inputs = refs[LEVELS + 2 : 2 * LEVELS + 2]
    (
        slow_send,
        slow_recv,
        fast_send,
        fast_recv,
        relay_buf,
        bias,
        trail,
        acc,
        e_send_buf,
        e_recv_buf,
    ) = refs[2 * LEVELS + 2 : 2 * LEVELS + 12]
    (
        threshold_ref,
        in_sem,
        edge_sem,
        slow_send_sem,
        slow_recv_sem,
        fast_send_sem,
        fast_recv_sem,
        relay_sem,
        e_send_sem,
        e_recv_sem,
        limit_sem,
        ready_sem,
    ) = refs[2 * LEVELS + 12 :]
    field_count, layers, width, _ = fields_ref.shape
    per_field = width // ROWS
    chunks = field_count * per_field
    devices = gz_count * xy_count
    stages = (gz_count - 1).bit_length()

    gz = lax.axis_index("gz")
    xy = lax.axis_index("xy")
    me = gz * xy_count + xy
    first = gz == 0
    last = gz == gz_count - 1
    even = lax.rem(gz, 2) == 0

    def wrapped(value, step, count):
        moved = value + step
        return jnp.where(moved >= count, moved - count, moved)

    def for_peers(act):
        for across in range(1, xy_count):
            act((gz, wrapped(xy, across, xy_count)))

        @pl.loop(1, gz_count)
        def _(along):
            for across in range(xy_count):
                act((wrapped(gz, along, gz_count), wrapped(xy, across, xy_count)))

    def for_both(step, act):
        @pl.when(gz >= step)
        def _():
            act(gz - step)

        @pl.when(gz < gz_count - step)
        def _():
            act(gz + step)

    def beside(step):
        return (gz >= step).astype(jnp.int32) + (gz < gz_count - step).astype(jnp.int32)

    barrier = pltpu.get_barrier_semaphore()

    def signal(sem, peer):
        pl.semaphore_signal(sem, inc=1, device_id=peer, device_id_type=MESH)

    for_both(1, lambda peer: signal(barrier, (peer, xy)))
    corner = jnp.logical_or(lax.rem(gz, 4) == 0, lax.rem(gz, 4) == 3)
    partner = jnp.where(even, gz + 3, gz - 3)
    if relay:

        @pl.when(corner)
        def _():
            signal(barrier, (partner, xy))

    for across in range(1, xy_count):
        signal(barrier, (gz, wrapped(xy, across, xy_count)))

    def ready_signal(k):
        if k < stages:
            for_both(1 << k, lambda peer: signal(ready_sem.at[k], (peer, xy)))

    def ready_wait(k):
        if k < stages:
            pl.semaphore_wait(ready_sem.at[k], beside(1 << k))

    def place(c):
        return c // per_field, pl.multiple_of(lax.rem(c, per_field) * ROWS, ROWS)

    def edge_copy(start, count):
        part = pl.ds(start, count)
        return pltpu.make_async_copy(fields_ref.at[:, part], inputs[0].at[:, part], edge_sem)

    def body_copy(c):
        f, row = place(c)
        where = (f, pl.ds(4, layers - 8), pl.ds(row, ROWS))
        return pltpu.make_async_copy(
            fields_ref.at[where], inputs[0].at[where], in_sem.at[c]
        )

    edge_copy(0, 4).start()
    edge_copy(layers - 4, 4).start()
    limit_copy = pltpu.make_async_copy(threshold_hbm, threshold_ref, limit_sem)
    limit_copy.start()

    @pl.loop(0, chunks)
    def _(c):
        body_copy(c).start()

    acc[...] = jnp.zeros_like(acc)

    def tiles(c):
        f, row = place(c)
        for t in range(ROWS // SUB):
            yield f, pl.ds(pl.multiple_of(row + t * SUB, SUB), SUB), pl.ds(t * SUB, SUB)

    def states_of(level, f, at, head):
        source = inputs[level]
        count = source.shape[1]
        make = head_states if head else tail_states
        return make(lambda j: source[f, j if j >= 0 else count + j, at])

    def put_states(buf, level, c, head):
        for f, at, to in tiles(c):
            one, two = states_of(level, f, at, head)
            buf[level, c, 0, to] = one
            buf[level, c, 1, to] = two

    units = LEVELS * chunks
    rows_between = gz_count // 4 - 1

    def by_relay(level, c, up, boundary):
        if up:
            share = (rows_between - boundary) * units // (rows_between + 1)
        else:
            share = (boundary + 1) * (boundary + 1) * units // (rows_between + 1) ** 2
        unit = level * chunks + c
        return (unit + 1) * share // units > unit * share // units

    def copy_of(send, recv, send_sem, recv_sem, level, c, peer):
        return pltpu.make_async_remote_copy(
            src_ref=send.at[level, c],
            dst_ref=recv.at[level, c],
            send_sem=send_sem,
            recv_sem=recv_sem,
            device_id={"gz": peer},
            device_id_type=MESH,
        )

    def lift(level, c, begin, end, low, high, emit_detail, emit_approx):
        source = inputs[level]
        half = source.shape[1] // 2
        final = level == LEVELS - 1
        limit = threshold_ref[c // per_field]

        def shrink(band):
            return band - jnp.minimum(jnp.maximum(band, -limit), limit)

        for f, at, to in tiles(c):
            evens = lambda i: source[f, 2 * i, at]
            odds = lambda i: source[f, 2 * i + 1, at]
            d1, s1, d2, sums = {}, {}, {}, {}

            def incoming(kind, which):
                if kind == "fast":
                    return fast_recv[level, c, which, to]
                if kind == "slow":
                    value = slow_recv[level, c, which, to]
                    return value + bias[c, which, to] if level else value
                return None

            def at_first(kind, mirrored, outer):
                return outer if kind == "fast" else jnp.where(first, mirrored, outer)

            def at_last(kind, mirrored, outer):
                outer = jnp.zeros_like(mirrored) if outer is None else outer
                return outer if kind == "fast" else jnp.where(last, mirrored, outer)

            def emit(kind, ref, i, value):
                band = shrink(value)
                ref[f, i, at] = band
                square = band * band
                sums[kind] = sums[kind] + square if kind in sums else square

            s = evens(begin)
            for i in range(begin, end + 1):
                if i < end:
                    if i + 1 < half:
                        s_next = evens(i + 1)
                    else:
                        s_next = at_last(high, s, incoming(high, 0))
                    d1[i] = odds(i) + ALPHA * (s + s_next)
                    if i == begin and low:
                        d1[i - 1] = at_first(low, d1[i], plus(incoming(low, 0), ALPHA * s))
                    if i - 1 in d1:
                        s1[i] = s + BETA * (d1[i - 1] + d1[i])
                    if i == begin and low:
                        s1[i - 1] = plus(incoming(low, 1), BETA * d1[i - 1])
                        d2[i - 1] = d1[i - 1] + GAMMA * (s1[i - 1] + s1[i])
                    s = s_next
                elif high:
                    s1[i] = at_last(high, s1[i - 1], plus(incoming(high, 1), BETA * d1[i - 1]))
                if i > begin and i - 1 in s1 and i in s1:
                    d2[i - 1] = d1[i - 1] + GAMMA * (s1[i - 1] + s1[i])
                    if i - 1 == begin and low:
                        d2[i - 2] = at_first(low, d2[i - 1], d2[i - 2])
                    if i - 1 in emit_detail:
                        emit(level, outs[level], i - 1, d2[i - 1] * (KAPPA / SQRT_TWO))
                    if i - 1 in emit_approx:
                        s2 = s1[i - 1] + DELTA * (d2[i - 2] + d2[i - 1])
                        approx = s2 * (SQRT_TWO / KAPPA)
                        if final:
                            emit(LEVELS, outs[LEVELS], i - 1, approx)
                        else:
                            inputs[level + 1][f, i - 1, at] = approx
            for kind, total in sums.items():
                acc[f, kind] += total

    lane = lax.broadcasted_iota(jnp.int32, (1, 128), 1)

    def reduced(f, row, kinds):
        for b in kinds:
            total = jnp.sum(jnp.sum(acc[f, b], axis=0, keepdims=True), axis=1, keepdims=True)
            row = jnp.where(lane == b, total, row)
        return row

    def analyse(head):
        slow_peer, fast_peer = (gz - 1, gz + 1) if head else (gz + 1, gz - 1)
        has_slow = gz > 0 if head else gz < gz_count - 1
        slow_copy = lambda level, c: copy_of(
            slow_send, slow_recv, slow_send_sem, slow_recv_sem.at[level, c], level, c, slow_peer
        )
        fast_copy = lambda level, c: copy_of(
            fast_send, fast_recv, fast_send_sem, fast_recv_sem.at[level % 2, c], level, c, fast_peer
        )
        touched = HEAD_TOUCHED if head else TAIL_TOUCHED
        far = (TRAIL_TAIL if head else TRAIL_HEAD)[1:] + ((3,) if head else (4,))
        top = LEVELS - 2

        def ends(slow, fast):
            return (slow, fast) if head else (fast, slow)

        relay_copy = lambda level, c: copy_of(
            slow_send, relay_buf, slow_send_sem, relay_sem.at[level, c], level, c, partner
        )
        onward = gz + 4 if head else gz - 4
        onward_copy = lambda level, c: copy_of(
            relay_buf, slow_recv, relay_sem.at[level, c], slow_recv_sem.at[level, c], level, c, onward
        )
        turn = jnp.logical_and(corner, has_slow)
        passes = jnp.logical_and(corner, gz < gz_count - 4 if head else gz >= 4)
        row = gz // 4

        def slow_start(level, c):
            if not relay:

                @pl.when(has_slow)
                def _():
                    slow_copy(level, c).start()

                return
            turned = jnp.logical_and(turn, by_relay(level, c, not head, row - 1 if head else row))

            @pl.when(turned)
            def _():
                relay_copy(level, c).start()

            @pl.when(jnp.logical_and(has_slow, jnp.logical_not(turned)))
            def _():
                slow_copy(level, c).start()

        def pass_on(level, c, act):
            if relay:
                passed = by_relay(level, c, head, row if head else row - 1)

                @pl.when(jnp.logical_and(passes, passed))
                def _():
                    act(level, c)

        def receive_and_send(level, c):
            relay_copy(level, c).wait_recv()
            onward_copy(level, c).start()

        def bulk(level, c):
            half = inputs[level].shape[1] // 2
            details, _ = touched[level]
            keep = range(max(details, 1), half - 2) if head else range(1, half - max(details, 2))
            lift(level, c, 0, half - 1, None, None, keep, range(2, half - 2))
            rim(level, c, head, "local", 0, 2)

        def rim(level, c, low_end, kind, details, approx):
            half = inputs[level].shape[1] // 2
            if low_end:
                lift(level, c, 0, approx + 1, kind, None, range(details), range(approx))
            else:
                begin = half - approx - 2
                span = lambda n: range(half - n, half)
                lift(level, c, begin, half, None, kind, span(details), span(approx))

        def fast_rim(level, c):
            if level < top:
                rim(level, c, not head, "fast", 2 if head else 1, 2)
            else:
                half = inputs[level].shape[1] // 2
                lift(level, c, 0, half, *ends("local", "fast"), range(0), range(half))

        def reach_back(level, c):
            count = (TRAIL_TAIL if head else TRAIL_HEAD)[level]
            for f, at, to in tiles(c):
                states = states_of(level, f, at, head)
                if head:
                    entry = lambda j: trail[c, -1 - j, to] if -count <= j < 0 else None
                else:
                    entry = lambda j: trail[c, j, to] if 0 <= j < count else None
                added = echo(entry, states, not head)
                keep = far[level]
                for n in range(keep):
                    trail[c, n, to] = added[-1 - n if head else n]
                after = lambda j: added[j] if (-1 - j if head else j) < keep else None
                one, two = (tail_states if head else head_states)(after)
                bias[c, 0, to] = one
                bias[c, 1, to] = two

        def settle(level, c):
            if level < top:
                rim(level, c, head, "slow", *touched[level])
            else:
                half = inputs[level].shape[1] // 2
                lift(level, c, 0, half, *ends("slow", "fast"), range(half), range(half))

        edge_copy(0, 8).wait()

        @pl.loop(0, chunks)
        def _(c):
            put_states(slow_send, 0, c, head)
            put_states(fast_send, 0, c, not head)

        limit_copy.wait()
        greeted = corner.astype(jnp.int32) if relay else 0
        pl.semaphore_wait(barrier, beside(1) + greeted + xy_count - 1)

        @pl.loop(0, chunks)
        def _(c):
            slow_start(0, c)
            fast_copy(0, c).start()

        ready_signal(0)

        @pl.loop(0, chunks)
        def _(c):
            body_copy(c).wait()
            bulk(0, c)
            put_states(slow_send, 1, c, head)
            slow_start(1, c)

        ready_wait(0)
        ready_signal(1)

        for level in range(top + 1):

            @pl.loop(0, chunks)
            def _(c):
                fast_copy(level, c).wait_recv()
                fast_rim(level, c)
                if level < top:
                    put_states(fast_send, level + 1, c, not head)
                    fast_copy(level + 1, c).start()
                if level + 1 < top:
                    bulk(level + 1, c)
                if level + 2 <= top:
                    put_states(slow_send, level + 2, c, head)
                    slow_start(level + 2, c)
                if level == top:
                    put_states(slow_send, top + 1, c, head)
                    slow_start(top + 1, c)

        ready_wait(1)
        ready_signal(2)
        if relay:

            @pl.loop(0, chunks)
            def _(c):
                for level in range(AHEAD):
                    pass_on(level, c, receive_and_send)

        for level in range(top + 1):
            if level:
                ready_wait(level + 1)
                ready_signal(level + 2)

            @pl.loop(0, chunks)
            def _(c):
                if level + AHEAD < LEVELS:
                    pass_on(level + AHEAD, c, receive_and_send)

                @pl.when(has_slow)
                def _():
                    slow_copy(level, c).wait_recv()

                settle(level, c)
                reach_back(level, c)
                if level == top:
                    put_states(fast_send, top + 1, c, not head)
                    fast_copy(top + 1, c).start()

        for stage in range(top + 2, stages):
            ready_wait(stage)
            ready_signal(stage + 1)

        zero = jnp.zeros((1, 128), jnp.float32)
        for f in range(field_count):
            e_send_buf[pl.ds(f, 1), :] = reduced(f, zero, range(top + 1))

        @pl.loop(0, chunks)
        def _(c):
            fast_copy(top + 1, c).wait_recv()

            @pl.when(has_slow)
            def _():
                slow_copy(top + 1, c).wait_recv()

            lift(top + 1, c, 0, 2, *ends("slow", "fast"), range(2), range(2))

        return lambda level, c: pass_on(level, c, lambda *at: onward_copy(*at).wait_send())

    def energy_copy(peer):
        return pltpu.make_async_remote_copy(
            src_ref=e_send_buf,
            dst_ref=e_recv_buf.at[me],
            send_sem=e_send_sem,
            recv_sem=e_recv_sem,
            device_id=peer,
            device_id_type=MESH,
        )

    def send_energies():
        for f in range(field_count):
            row = e_send_buf[pl.ds(f, 1), :]
            e_send_buf[pl.ds(f, 1), :] = reduced(f, row, range(LEVELS - 1, LEVELS + 1))
        for_peers(lambda peer: energy_copy(peer).start())

    def whole(head):
        finish = analyse(head)
        send_energies()
        if relay:

            @pl.loop(0, chunks)
            def _(c):
                for level in range(LEVELS):
                    finish(level, c)

    @pl.when(even)
    def _():
        whole(True)

    @pl.when(jnp.logical_not(even))
    def _():
        whole(False)

    e_recv_buf[me] = e_send_buf[...]

    pltpu.make_async_copy(fast_send, fast_send, fast_send_sem).wait()

    @pl.when(jnp.where(even, gz > 0, gz < gz_count - 1))
    def _():
        pltpu.make_async_copy(slow_send, slow_send, slow_send_sem).wait()

    others = e_recv_buf.at[pl.ds(0, devices - 1)]
    pltpu.make_async_copy(others, others, e_recv_sem).wait()

    totals = jnp.sum(e_recv_buf[...], axis=0)
    cells = jnp.ones((1, 128), jnp.float32)
    for b in range(LEVELS + 1):
        shape = outs[b].shape
        cells = jnp.where(lane == b, float(shape[1] * shape[2] * shape[3] * devices), cells)
    energy_ref[...] = (totals / cells)[:, : LEVELS + 1]

    pltpu.make_async_copy(others, others, e_send_sem).wait()


def write_out(*refs):
    count = (len(refs) - 1) // 2
    sources, targets, sems = refs[:count], refs[count : 2 * count], refs[-1]
    copies = [
        pltpu.make_async_copy(source, target, sems.at[k])
        for k, (source, target) in enumerate(zip(sources, targets))
    ]
    for copy in copies:
        copy.start()
    for copy in copies:
        copy.wait()


def zigzag(mesh):
    line = [getattr(device, "coords", None) for device in mesh.devices[:, 0]]
    if len(line) % 4 or None in line:
        return False
    apart = lambda a, b: sum(abs(p - q) for p, q in zip(line[a], line[b]))
    return all(
        (apart(g, g + 1), apart(g, g - 3), apart(g - 3, g + 1), apart(g + 1, g + 4), apart(g + 4, g))
        == (2, 1, 1, 1, 1)
        for g in range(3, len(line) - 1, 4)
    )


def solution(mesh):
    relay = zigzag(mesh)
    gz_count, xy_count = mesh.shape["gz"], mesh.shape["xy"]
    devices = gz_count * xy_count

    def local(fields, threshold):
        field_count, layers, width, depth = fields.shape
        chunks = field_count * (width // ROWS)
        assert gz_count % 2 == 0 and layers >> (LEVELS - 2) == 8
        f32 = jnp.float32
        halves = [layers >> (level + 1) for level in range(LEVELS)]
        band_layers = halves + halves[-1:]
        vmem = pl.BlockSpec(memory_space=pltpu.VMEM)
        shapes = tuple(
            jax.ShapeDtypeStruct((field_count, n, width, depth), f32) for n in band_layers
        ) + (jax.ShapeDtypeStruct((field_count, LEVELS + 1), f32),)
        results = pl.pallas_call(
            functools.partial(kernel, gz_count, xy_count, relay),
            out_shape=tuple(pltpu.VMEM(shape.shape, shape.dtype) for shape in shapes),
            in_specs=[
                pl.BlockSpec(memory_space=pltpu.HBM),
                pl.BlockSpec(memory_space=pltpu.HBM),
            ],
            out_specs=(vmem,) * (LEVELS + 2),
            scratch_shapes=[
                pltpu.VMEM((field_count, n, width, depth), f32) for n in [layers] + halves[:-1]
            ]
            + [
                pltpu.VMEM((LEVELS, chunks, 2, ROWS, depth), f32),
                pltpu.VMEM((LEVELS, chunks, 2, ROWS, depth), f32),
                pltpu.VMEM((LEVELS, chunks, 2, ROWS, depth), f32),
                pltpu.VMEM((LEVELS, chunks, 2, ROWS, depth), f32),
                pltpu.VMEM((LEVELS, chunks, 2, ROWS, depth), f32),
                pltpu.VMEM((chunks, 2, ROWS, depth), f32),
                pltpu.VMEM((chunks, 4, ROWS, depth), f32),
                pltpu.VMEM((field_count, LEVELS + 1, SUB, depth), f32),
                pltpu.VMEM((field_count, 128), f32),
                pltpu.VMEM((devices, field_count, 128), f32),
                pltpu.SMEM((field_count,), f32),
                pltpu.SemaphoreType.DMA((chunks,)),
                pltpu.SemaphoreType.DMA,
                pltpu.SemaphoreType.DMA,
                pltpu.SemaphoreType.DMA((LEVELS, chunks)),
                pltpu.SemaphoreType.DMA,
                pltpu.SemaphoreType.DMA((2, chunks)),
                pltpu.SemaphoreType.DMA((LEVELS, chunks)),
                pltpu.SemaphoreType.DMA,
                pltpu.SemaphoreType.DMA,
                pltpu.SemaphoreType.DMA,
                pltpu.SemaphoreType.REGULAR(((gz_count - 1).bit_length(),)),
            ],
            compiler_params=pltpu.CompilerParams(
                collective_id=0,
                has_side_effects=True,
                vmem_limit_bytes=32 * 1024 * 1024,
            ),
        )(
            pltpu.with_memory_space_constraint(threshold, pltpu.HBM),
            pltpu.with_memory_space_constraint(fields, pltpu.HBM),
        )
        return pl.pallas_call(
            write_out,
            out_shape=shapes,
            in_specs=[vmem] * (LEVELS + 2),
            out_specs=(pl.BlockSpec(memory_space=pltpu.HBM),) * (LEVELS + 2),
            scratch_shapes=[pltpu.SemaphoreType.DMA((LEVELS + 2,))],
            compiler_params=pltpu.CompilerParams(vmem_limit_bytes=4 * 1024 * 1024),
        )(*(pltpu.with_memory_space_constraint(result, pltpu.VMEM) for result in results))

    banded = P(None, "gz", "xy", None)
    return jax.shard_map(
        local,
        mesh=mesh,
        in_specs=(banded, P()),
        out_specs=(banded,) * (LEVELS + 1) + (P(),),
        check_vma=False,
    )
```

```python
import functools

import jax
import jax.numpy as jnp
from jax import lax
from jax.experimental import pallas as pl
from jax.experimental.pallas import tpu as pltpu
from jax.sharding import PartitionSpec as P

ALPHA = -1.586134342059924
BETA = -0.052980118572961
GAMMA = 0.882911075530934
DELTA = 0.443506852043971
KAPPA = 1.230174104914001
SQRT_TWO = 1.4142135623730951
LEVELS = 5
MESH = pl.DeviceIdType.MESH
SUB = 8
ROWS = 32
AHEAD = 2


def plus(*terms):
    terms = [term for term in terms if term is not None]
    return functools.reduce(lambda x, y: x + y, terms) if terms else None


def times(factor, value):
    return None if value is None else factor * value


def head_states(entry):
    s_head, d_head, s_after = (entry(j) for j in range(3))
    d_lifted = plus(d_head, times(ALPHA, plus(s_head, s_after)))
    return s_head, plus(s_head, times(BETA, d_lifted))


def tail_states(entry):
    s_prev, d_prev, s_tail, d_tail = (entry(j) for j in range(-4, 0))
    d_lifted = plus(d_prev, times(ALPHA, plus(s_prev, s_tail)))
    return plus(d_tail, times(ALPHA, s_tail)), plus(s_tail, times(BETA, d_lifted))


def echo(entry, states, head):
    reach = range(-1, 4) if head else range(-4, 1)
    inside = (lambda j: j >= 0) if head else (lambda j: j < 0)
    s = {j: entry(2 * j) for j in reach if inside(j)}
    d = {j: entry(2 * j + 1) for j in reach if inside(j)}
    if not head:
        s[0] = states[0]
    d1, s1, d2, s2 = {}, {}, {}, {}
    for j in reach:
        if inside(j):
            d1[j] = plus(d.get(j), times(ALPHA, plus(s.get(j), s.get(j + 1))))
    if head:
        d1[-1] = plus(states[0], times(ALPHA, s[0]))
    for j in reach:
        if inside(j):
            s1[j] = plus(s.get(j), times(BETA, plus(d1.get(j - 1), d1.get(j))))
    beyond = -1 if head else 0
    s1[beyond] = plus(states[1], times(BETA, d1[-1]))
    for j in range(-1, 4) if head else range(-4, 0):
        d2[j] = plus(d1.get(j), times(GAMMA, plus(s1.get(j), s1.get(j + 1))))
    for j in reach:
        if inside(j):
            s2[j] = plus(s1.get(j), times(DELTA, plus(d2.get(j - 1), d2.get(j))))
    return {j: times(SQRT_TWO / KAPPA, value) for j, value in s2.items() if value is not None}


HEAD_TOUCHED = ((1, 2), (2, 3), (3, 4))
TAIL_TOUCHED = ((2, 2), (3, 3), (3, 3))
TRAIL_HEAD = (0, 2, 3, 4)
TRAIL_TAIL = (0, 2, 3, 3)


def kernel(
    gz_count,
    xy_count,
    relay,
    threshold_hbm,
    fields_ref,
    *refs,
):
    outs = refs[: LEVELS + 1]
    energy_ref = refs[LEVELS + 1]
    inputs = refs[LEVELS + 2 : 2 * LEVELS + 2]
    (
        slow_send,
        slow_recv,
        fast_send,
        fast_recv,
        relay_buf,
        bias,
        trail,
        acc,
        e_send_buf,
        e_recv_buf,
    ) = refs[2 * LEVELS + 2 : 2 * LEVELS + 12]
    (
        threshold_ref,
        in_sem,
        edge_sem,
        slow_send_sem,
        slow_recv_sem,
        fast_send_sem,
        fast_recv_sem,
        relay_sem,
        e_send_sem,
        e_recv_sem,
        limit_sem,
        ready_sem,
    ) = refs[2 * LEVELS + 12 :]
    field_count, layers, width, _ = fields_ref.shape
    per_field = width // ROWS
    chunks = field_count * per_field
    devices = gz_count * xy_count
    stages = (gz_count - 1).bit_length()

    gz = lax.axis_index("gz")
    xy = lax.axis_index("xy")
    me = gz * xy_count + xy
    first = gz == 0
    last = gz == gz_count - 1
    even = lax.rem(gz, 2) == 0

    def wrapped(value, step, count):
        moved = value + step
        return jnp.where(moved >= count, moved - count, moved)

    def for_peers(act):
        @pl.loop(0, gz_count)
        def _(along):
            for across in range(xy_count):

                @pl.when(jnp.logical_or(along != gz, xy != across))
                def _():
                    act((along, across))

    def for_both(step, act):
        @pl.when(gz >= step)
        def _():
            act(gz - step)

        @pl.when(gz < gz_count - step)
        def _():
            act(gz + step)

    def beside(step):
        return (gz >= step).astype(jnp.int32) + (gz < gz_count - step).astype(jnp.int32)

    barrier = pltpu.get_barrier_semaphore()

    def signal(sem, peer):
        pl.semaphore_signal(sem, inc=1, device_id=peer, device_id_type=MESH)

    for_both(1, lambda peer: signal(barrier, (peer, xy)))
    corner = jnp.logical_or(lax.rem(gz, 4) == 0, lax.rem(gz, 4) == 3)
    partner = jnp.where(even, gz + 3, gz - 3)
    if relay:

        @pl.when(corner)
        def _():
            signal(barrier, (partner, xy))

    for across in range(1, xy_count):
        signal(barrier, (gz, wrapped(xy, across, xy_count)))

    def ready_signal(k):
        if k < stages:
            for_both(1 << k, lambda peer: signal(ready_sem.at[k], (peer, xy)))

    def ready_wait(k):
        if k < stages:
            pl.semaphore_wait(ready_sem.at[k], beside(1 << k))

    def place(c):
        return c // per_field, pl.multiple_of(lax.rem(c, per_field) * ROWS, ROWS)

    def edge_copy(start, count):
        part = pl.ds(start, count)
        return pltpu.make_async_copy(fields_ref.at[:, part], inputs[0].at[:, part], edge_sem)

    def body_copy(c):
        f, row = place(c)
        where = (f, pl.ds(4, layers - 8), pl.ds(row, ROWS))
        return pltpu.make_async_copy(
            fields_ref.at[where], inputs[0].at[where], in_sem.at[c]
        )

    edge_copy(0, 4).start()
    edge_copy(layers - 4, 4).start()
    limit_copy = pltpu.make_async_copy(threshold_hbm, threshold_ref, limit_sem)
    limit_copy.start()

    @pl.loop(0, chunks)
    def _(c):
        body_copy(c).start()

    acc[...] = jnp.zeros_like(acc)

    def tiles(c):
        f, row = place(c)
        for t in range(ROWS // SUB):
            yield f, pl.ds(pl.multiple_of(row + t * SUB, SUB), SUB), pl.ds(t * SUB, SUB)

    def states_of(level, f, at, head):
        source = inputs[level]
        count = source.shape[1]
        make = head_states if head else tail_states
        return make(lambda j: source[f, j if j >= 0 else count + j, at])

    def put_states(buf, level, c, head):
        for f, at, to in tiles(c):
            one, two = states_of(level, f, at, head)
            buf[level, c, 0, to] = one
            buf[level, c, 1, to] = two

    units = LEVELS * chunks
    rows_between = gz_count // 4 - 1

    def by_relay(level, c, up, boundary):
        if up:
            share = (2 * (rows_between - boundary) + 1) * units // (2 * rows_between + 4)
        else:
            whole = 2 * (rows_between + 1) ** 2
            share = (2 * (boundary + 1) * (boundary + 1) * units + whole // 2 - 1) // whole
        unit = level * chunks + c
        return (unit + 1) * share // units > unit * share // units

    def copy_of(send, recv, send_sem, recv_sem, level, c, peer):
        return pltpu.make_async_remote_copy(
            src_ref=send.at[level, c],
            dst_ref=recv.at[level, c],
            send_sem=send_sem,
            recv_sem=recv_sem,
            device_id={"gz": peer},
            device_id_type=MESH,
        )

    def lift(level, c, begin, end, low, high, emit_detail, emit_approx):
        source = inputs[level]
        half = source.shape[1] // 2
        final = level == LEVELS - 1
        limit = threshold_ref[c // per_field]

        def shrink(band):
            return band - jnp.minimum(jnp.maximum(band, -limit), limit)

        for f, at, to in tiles(c):
            evens = lambda i: source[f, 2 * i, at]
            odds = lambda i: source[f, 2 * i + 1, at]
            d1, s1, d2, sums = {}, {}, {}, {}

            def incoming(kind, which):
                if kind == "fast":
                    return fast_recv[level, c, which, to]
                if kind == "slow":
                    value = slow_recv[level, c, which, to]
                    return value + bias[c, which, to] if level else value
                return None

            def at_first(kind, mirrored, outer):
                return outer if kind == "fast" else jnp.where(first, mirrored, outer)

            def at_last(kind, mirrored, outer):
                outer = jnp.zeros_like(mirrored) if outer is None else outer
                return outer if kind == "fast" else jnp.where(last, mirrored, outer)

            def emit(kind, ref, i, value):
                band = shrink(value)
                ref[f, i, at] = band
                square = band * band
                sums[kind] = sums[kind] + square if kind in sums else square

            s = evens(begin)
            for i in range(begin, end + 1):
                if i < end:
                    if i + 1 < half:
                        s_next = evens(i + 1)
                    else:
                        s_next = at_last(high, s, incoming(high, 0))
                    d1[i] = odds(i) + ALPHA * (s + s_next)
                    if i == begin and low:
                        d1[i - 1] = at_first(low, d1[i], plus(incoming(low, 0), ALPHA * s))
                    if i - 1 in d1:
                        s1[i] = s + BETA * (d1[i - 1] + d1[i])
                    if i == begin and low:
                        s1[i - 1] = plus(incoming(low, 1), BETA * d1[i - 1])
                        d2[i - 1] = d1[i - 1] + GAMMA * (s1[i - 1] + s1[i])
                    s = s_next
                elif high:
                    s1[i] = at_last(high, s1[i - 1], plus(incoming(high, 1), BETA * d1[i - 1]))
                if i > begin and i - 1 in s1 and i in s1:
                    d2[i - 1] = d1[i - 1] + GAMMA * (s1[i - 1] + s1[i])
                    if i - 1 == begin and low:
                        d2[i - 2] = at_first(low, d2[i - 1], d2[i - 2])
                    if i - 1 in emit_detail:
                        emit(level, outs[level], i - 1, d2[i - 1] * (KAPPA / SQRT_TWO))
                    if i - 1 in emit_approx:
                        s2 = s1[i - 1] + DELTA * (d2[i - 2] + d2[i - 1])
                        approx = s2 * (SQRT_TWO / KAPPA)
                        if final:
                            emit(LEVELS, outs[LEVELS], i - 1, approx)
                        else:
                            inputs[level + 1][f, i - 1, at] = approx
            for kind, total in sums.items():
                acc[f, kind] += total

    lane = lax.broadcasted_iota(jnp.int32, (1, 128), 1)

    def reduced(f, row, kinds):
        for b in kinds:
            total = jnp.sum(jnp.sum(acc[f, b], axis=0, keepdims=True), axis=1, keepdims=True)
            row = jnp.where(lane == b, total, row)
        return row

    def analyse(head):
        slow_peer, fast_peer = (gz - 1, gz + 1) if head else (gz + 1, gz - 1)
        has_slow = gz > 0 if head else gz < gz_count - 1
        slow_copy = lambda level, c: copy_of(
            slow_send, slow_recv, slow_send_sem, slow_recv_sem.at[level, c], level, c, slow_peer
        )
        fast_copy = lambda level, c: copy_of(
            fast_send, fast_recv, fast_send_sem, fast_recv_sem.at[level % 2, c], level, c, fast_peer
        )
        touched = HEAD_TOUCHED if head else TAIL_TOUCHED
        far = (TRAIL_TAIL if head else TRAIL_HEAD)[1:] + ((3,) if head else (4,))
        top = LEVELS - 2

        def ends(slow, fast):
            return (slow, fast) if head else (fast, slow)

        relay_copy = lambda level, c: copy_of(
            slow_send, relay_buf, slow_send_sem, relay_sem.at[level, c], level, c, partner
        )
        onward = gz + 4 if head else gz - 4
        onward_copy = lambda level, c: copy_of(
            relay_buf, slow_recv, relay_sem.at[level, c], slow_recv_sem.at[level, c], level, c, onward
        )
        turn = jnp.logical_and(corner, has_slow)
        passes = jnp.logical_and(corner, gz < gz_count - 4 if head else gz >= 4)
        row = gz // 4

        def slow_start(level, c):
            if not relay:

                @pl.when(has_slow)
                def _():
                    slow_copy(level, c).start()

                return
            turned = jnp.logical_and(turn, by_relay(level, c, not head, row - 1 if head else row))

            @pl.when(turned)
            def _():
                relay_copy(level, c).start()

            @pl.when(jnp.logical_and(has_slow, jnp.logical_not(turned)))
            def _():
                slow_copy(level, c).start()

        def pass_on(level, c, act):
            if relay:
                passed = by_relay(level, c, head, row if head else row - 1)

                @pl.when(jnp.logical_and(passes, passed))
                def _():
                    act(level, c)

        def receive_and_send(level, c):
            relay_copy(level, c).wait_recv()
            onward_copy(level, c).start()

        def bulk(level, c):
            half = inputs[level].shape[1] // 2
            details, _ = touched[level]
            keep = range(max(details, 1), half - 2) if head else range(1, half - max(details, 2))
            lift(level, c, 0, half - 1, None, None, keep, range(2, half - 2))
            rim(level, c, head, "local", 0, 2)

        def rim(level, c, low_end, kind, details, approx):
            half = inputs[level].shape[1] // 2
            if low_end:
                lift(level, c, 0, approx + 1, kind, None, range(details), range(approx))
            else:
                begin = half - approx - 2
                span = lambda n: range(half - n, half)
                lift(level, c, begin, half, None, kind, span(details), span(approx))

        def fast_rim(level, c):
            if level < top:
                rim(level, c, not head, "fast", 2 if head else 1, 2)
            else:
                half = inputs[level].shape[1] // 2
                lift(level, c, 0, half, *ends("local", "fast"), range(0), range(half))

        def reach_back(level, c):
            count = (TRAIL_TAIL if head else TRAIL_HEAD)[level]
            for f, at, to in tiles(c):
                states = states_of(level, f, at, head)
                if head:
                    entry = lambda j: trail[c, -1 - j, to] if -count <= j < 0 else None
                else:
                    entry = lambda j: trail[c, j, to] if 0 <= j < count else None
                added = echo(entry, states, not head)
                keep = far[level]
                for n in range(keep):
                    trail[c, n, to] = added[-1 - n if head else n]
                after = lambda j: added[j] if (-1 - j if head else j) < keep else None
                one, two = (tail_states if head else head_states)(after)
                bias[c, 0, to] = one
                bias[c, 1, to] = two

        def settle(level, c):
            if level < top:
                rim(level, c, head, "slow", *touched[level])
            else:
                half = inputs[level].shape[1] // 2
                lift(level, c, 0, half, *ends("slow", "fast"), range(half), range(half))

        edge_copy(0, 8).wait()

        @pl.loop(0, chunks)
        def _(c):
            put_states(slow_send, 0, c, head)
            put_states(fast_send, 0, c, not head)

        limit_copy.wait()
        greeted = corner.astype(jnp.int32) if relay else 0
        pl.semaphore_wait(barrier, beside(1) + greeted + xy_count - 1)

        @pl.loop(0, chunks)
        def _(c):
            slow_start(0, c)
            fast_copy(0, c).start()

        ready_signal(0)

        @pl.loop(0, chunks)
        def _(c):
            body_copy(c).wait()
            bulk(0, c)
            put_states(slow_send, 1, c, head)
            slow_start(1, c)

        ready_wait(0)
        ready_signal(1)

        for level in range(top + 1):

            @pl.loop(0, chunks)
            def _(c):
                fast_copy(level, c).wait_recv()
                fast_rim(level, c)
                if level < top:
                    put_states(fast_send, level + 1, c, not head)
                    fast_copy(level + 1, c).start()
                if level + 1 < top:
                    bulk(level + 1, c)
                if level + 2 <= top:
                    put_states(slow_send, level + 2, c, head)
                    slow_start(level + 2, c)
                if level == top:
                    put_states(slow_send, top + 1, c, head)
                    slow_start(top + 1, c)

        ready_wait(1)
        ready_signal(2)
        if relay:

            @pl.loop(0, chunks)
            def _(c):
                for level in range(AHEAD):
                    pass_on(level, c, receive_and_send)

        for level in range(top + 1):
            if level:
                ready_wait(level + 1)
                ready_signal(level + 2)

            @pl.loop(0, chunks)
            def _(c):
                if level + AHEAD < LEVELS:
                    pass_on(level + AHEAD, c, receive_and_send)

                @pl.when(has_slow)
                def _():
                    slow_copy(level, c).wait_recv()

                settle(level, c)
                reach_back(level, c)
                if level == top:
                    put_states(fast_send, top + 1, c, not head)
                    fast_copy(top + 1, c).start()

        for stage in range(top + 2, stages):
            ready_wait(stage)
            ready_signal(stage + 1)

        zero = jnp.zeros((1, 128), jnp.float32)
        for f in range(field_count):
            e_send_buf[pl.ds(f, 1), :] = reduced(f, zero, range(top + 1))

        @pl.loop(0, chunks)
        def _(c):
            fast_copy(top + 1, c).wait_recv()

            @pl.when(has_slow)
            def _():
                slow_copy(top + 1, c).wait_recv()

            lift(top + 1, c, 0, 2, *ends("slow", "fast"), range(2), range(2))

        return lambda level, c: pass_on(level, c, lambda *at: onward_copy(*at).wait_send())

    def energy_copy(peer):
        return pltpu.make_async_remote_copy(
            src_ref=e_send_buf,
            dst_ref=e_recv_buf.at[me],
            send_sem=e_send_sem,
            recv_sem=e_recv_sem,
            device_id=peer,
            device_id_type=MESH,
        )

    def send_energies():
        for f in range(field_count):
            row = e_send_buf[pl.ds(f, 1), :]
            e_send_buf[pl.ds(f, 1), :] = reduced(f, row, range(LEVELS - 1, LEVELS + 1))
        for_peers(lambda peer: energy_copy(peer).start())

    def whole(head):
        finish = analyse(head)
        send_energies()
        if relay:

            @pl.loop(0, chunks)
            def _(c):
                for level in range(LEVELS):
                    finish(level, c)

    @pl.when(even)
    def _():
        whole(True)

    @pl.when(jnp.logical_not(even))
    def _():
        whole(False)

    e_recv_buf[me] = e_send_buf[...]

    pltpu.make_async_copy(fast_send, fast_send, fast_send_sem).wait()

    @pl.when(jnp.where(even, gz > 0, gz < gz_count - 1))
    def _():
        pltpu.make_async_copy(slow_send, slow_send, slow_send_sem).wait()

    others = e_recv_buf.at[pl.ds(0, devices - 1)]
    pltpu.make_async_copy(others, others, e_recv_sem).wait()

    totals = jnp.sum(e_recv_buf[...], axis=0)
    cells = jnp.ones((1, 128), jnp.float32)
    for b in range(LEVELS + 1):
        shape = outs[b].shape
        cells = jnp.where(lane == b, float(shape[1] * shape[2] * shape[3] * devices), cells)
    energy_ref[...] = (totals / cells)[:, : LEVELS + 1]

    pltpu.make_async_copy(others, others, e_send_sem).wait()


def write_out(*refs):
    count = (len(refs) - 1) // 2
    sources, targets, sems = refs[:count], refs[count : 2 * count], refs[-1]
    copies = [
        pltpu.make_async_copy(source, target, sems.at[k])
        for k, (source, target) in enumerate(zip(sources, targets))
    ]
    for copy in copies:
        copy.start()
    for copy in copies:
        copy.wait()


def zigzag(mesh):
    line = [getattr(device, "coords", None) for device in mesh.devices[:, 0]]
    if len(line) % 4 or None in line:
        return False
    apart = lambda a, b: sum(abs(p - q) for p, q in zip(line[a], line[b]))
    return all(
        (apart(g, g + 1), apart(g, g - 3), apart(g - 3, g + 1), apart(g + 1, g + 4), apart(g + 4, g))
        == (2, 1, 1, 1, 1)
        for g in range(3, len(line) - 1, 4)
    )


def solution(mesh):
    relay = zigzag(mesh)
    gz_count, xy_count = mesh.shape["gz"], mesh.shape["xy"]
    devices = gz_count * xy_count

    def local(fields, threshold):
        field_count, layers, width, depth = fields.shape
        chunks = field_count * (width // ROWS)
        assert gz_count % 2 == 0 and layers >> (LEVELS - 2) == 8
        f32 = jnp.float32
        halves = [layers >> (level + 1) for level in range(LEVELS)]
        band_layers = halves + halves[-1:]
        vmem = pl.BlockSpec(memory_space=pltpu.VMEM)
        shapes = tuple(
            jax.ShapeDtypeStruct((field_count, n, width, depth), f32) for n in band_layers
        ) + (jax.ShapeDtypeStruct((field_count, LEVELS + 1), f32),)
        results = pl.pallas_call(
            functools.partial(kernel, gz_count, xy_count, relay),
            out_shape=tuple(pltpu.VMEM(shape.shape, shape.dtype) for shape in shapes),
            in_specs=[
                pl.BlockSpec(memory_space=pltpu.HBM),
                pl.BlockSpec(memory_space=pltpu.HBM),
            ],
            out_specs=(vmem,) * (LEVELS + 2),
            scratch_shapes=[
                pltpu.VMEM((field_count, n, width, depth), f32) for n in [layers] + halves[:-1]
            ]
            + [
                pltpu.VMEM((LEVELS, chunks, 2, ROWS, depth), f32),
                pltpu.VMEM((LEVELS, chunks, 2, ROWS, depth), f32),
                pltpu.VMEM((LEVELS, chunks, 2, ROWS, depth), f32),
                pltpu.VMEM((LEVELS, chunks, 2, ROWS, depth), f32),
                pltpu.VMEM((LEVELS, chunks, 2, ROWS, depth), f32),
                pltpu.VMEM((chunks, 2, ROWS, depth), f32),
                pltpu.VMEM((chunks, 4, ROWS, depth), f32),
                pltpu.VMEM((field_count, LEVELS + 1, SUB, depth), f32),
                pltpu.VMEM((field_count, 128), f32),
                pltpu.VMEM((devices, field_count, 128), f32),
                pltpu.SMEM((field_count,), f32),
                pltpu.SemaphoreType.DMA((chunks,)),
                pltpu.SemaphoreType.DMA,
                pltpu.SemaphoreType.DMA,
                pltpu.SemaphoreType.DMA((LEVELS, chunks)),
                pltpu.SemaphoreType.DMA,
                pltpu.SemaphoreType.DMA((2, chunks)),
                pltpu.SemaphoreType.DMA((LEVELS, chunks)),
                pltpu.SemaphoreType.DMA,
                pltpu.SemaphoreType.DMA,
                pltpu.SemaphoreType.DMA,
                pltpu.SemaphoreType.REGULAR(((gz_count - 1).bit_length(),)),
            ],
            compiler_params=pltpu.CompilerParams(
                collective_id=0,
                has_side_effects=True,
                vmem_limit_bytes=32 * 1024 * 1024,
            ),
        )(
            pltpu.with_memory_space_constraint(threshold, pltpu.HBM),
            pltpu.with_memory_space_constraint(fields, pltpu.HBM),
        )
        return pl.pallas_call(
            write_out,
            out_shape=shapes,
            in_specs=[vmem] * (LEVELS + 2),
            out_specs=(pl.BlockSpec(memory_space=pltpu.HBM),) * (LEVELS + 2),
            scratch_shapes=[pltpu.SemaphoreType.DMA((LEVELS + 2,))],
            compiler_params=pltpu.CompilerParams(vmem_limit_bytes=4 * 1024 * 1024),
        )(*(pltpu.with_memory_space_constraint(result, pltpu.VMEM) for result in results))

    banded = P(None, "gz", "xy", None)
    return jax.shard_map(
        local,
        mesh=mesh,
        in_specs=(banded, P()),
        out_specs=(banded,) * (LEVELS + 1) + (P(),),
        check_vma=False,
    )
```

```python
import functools

import jax
import jax.numpy as jnp
from jax import lax
from jax.experimental import pallas as pl
from jax.experimental.pallas import tpu as pltpu
from jax.sharding import PartitionSpec as P

ALPHA = -1.586134342059924
BETA = -0.052980118572961
GAMMA = 0.882911075530934
DELTA = 0.443506852043971
KAPPA = 1.230174104914001
SQRT_TWO = 1.4142135623730951
LEVELS = 5
MESH = pl.DeviceIdType.MESH
SUB = 8
ROWS = 32
AHEAD = 2
LATE = 1


def plus(*terms):
    terms = [term for term in terms if term is not None]
    return functools.reduce(lambda x, y: x + y, terms) if terms else None


def times(factor, value):
    return None if value is None else factor * value


def head_states(entry):
    s_head, d_head, s_after = (entry(j) for j in range(3))
    d_lifted = plus(d_head, times(ALPHA, plus(s_head, s_after)))
    return s_head, plus(s_head, times(BETA, d_lifted))


def tail_states(entry):
    s_prev, d_prev, s_tail, d_tail = (entry(j) for j in range(-4, 0))
    d_lifted = plus(d_prev, times(ALPHA, plus(s_prev, s_tail)))
    return plus(d_tail, times(ALPHA, s_tail)), plus(s_tail, times(BETA, d_lifted))


def echo(entry, states, head):
    reach = range(-1, 4) if head else range(-4, 1)
    inside = (lambda j: j >= 0) if head else (lambda j: j < 0)
    s = {j: entry(2 * j) for j in reach if inside(j)}
    d = {j: entry(2 * j + 1) for j in reach if inside(j)}
    if not head:
        s[0] = states[0]
    d1, s1, d2, s2 = {}, {}, {}, {}
    for j in reach:
        if inside(j):
            d1[j] = plus(d.get(j), times(ALPHA, plus(s.get(j), s.get(j + 1))))
    if head:
        d1[-1] = plus(states[0], times(ALPHA, s[0]))
    for j in reach:
        if inside(j):
            s1[j] = plus(s.get(j), times(BETA, plus(d1.get(j - 1), d1.get(j))))
    beyond = -1 if head else 0
    s1[beyond] = plus(states[1], times(BETA, d1[-1]))
    for j in range(-1, 4) if head else range(-4, 0):
        d2[j] = plus(d1.get(j), times(GAMMA, plus(s1.get(j), s1.get(j + 1))))
    for j in reach:
        if inside(j):
            s2[j] = plus(s1.get(j), times(DELTA, plus(d2.get(j - 1), d2.get(j))))
    return {j: times(SQRT_TWO / KAPPA, value) for j, value in s2.items() if value is not None}


HEAD_TOUCHED = ((1, 2), (2, 3), (3, 4))
TAIL_TOUCHED = ((2, 2), (3, 3), (3, 3))
TRAIL_HEAD = (0, 2, 3, 4)
TRAIL_TAIL = (0, 2, 3, 3)


def kernel(
    gz_count,
    xy_count,
    relay,
    threshold_hbm,
    fields_ref,
    *refs,
):
    outs = refs[: LEVELS + 1]
    energy_ref = refs[LEVELS + 1]
    inputs = refs[LEVELS + 2 : 2 * LEVELS + 2]
    (
        slow_send,
        slow_recv,
        fast_send,
        fast_recv,
        relay_buf,
        bias,
        trail,
        acc,
        e_send_buf,
        e_recv_buf,
    ) = refs[2 * LEVELS + 2 : 2 * LEVELS + 12]
    (
        threshold_ref,
        in_sem,
        edge_sem,
        slow_send_sem,
        slow_recv_sem,
        fast_send_sem,
        fast_recv_sem,
        relay_sem,
        e_send_sem,
        e_recv_sem,
        limit_sem,
        ready_sem,
    ) = refs[2 * LEVELS + 12 :]
    field_count, layers, width, _ = fields_ref.shape
    per_field = width // ROWS
    chunks = field_count * per_field
    devices = gz_count * xy_count
    stages = (gz_count - 1).bit_length()

    gz = lax.axis_index("gz")
    xy = lax.axis_index("xy")
    me = gz * xy_count + xy
    first = gz == 0
    last = gz == gz_count - 1
    even = lax.rem(gz, 2) == 0

    def wrapped(value, step, count):
        moved = value + step
        return jnp.where(moved >= count, moved - count, moved)

    def for_peers(act):
        @pl.loop(0, gz_count)
        def _(along):
            for across in range(xy_count):

                @pl.when(jnp.logical_or(along != gz, xy != across))
                def _():
                    act((along, across))

    def for_both(step, act):
        @pl.when(gz >= step)
        def _():
            act(gz - step)

        @pl.when(gz < gz_count - step)
        def _():
            act(gz + step)

    def beside(step):
        return (gz >= step).astype(jnp.int32) + (gz < gz_count - step).astype(jnp.int32)

    barrier = pltpu.get_barrier_semaphore()

    def signal(sem, peer):
        pl.semaphore_signal(sem, inc=1, device_id=peer, device_id_type=MESH)

    for_both(1, lambda peer: signal(barrier, (peer, xy)))
    corner = jnp.logical_or(lax.rem(gz, 4) == 0, lax.rem(gz, 4) == 3)
    partner = jnp.where(even, gz + 3, gz - 3)
    if relay:

        @pl.when(corner)
        def _():
            signal(barrier, (partner, xy))

    for across in range(1, xy_count):
        signal(barrier, (gz, wrapped(xy, across, xy_count)))

    def ready_signal(k):
        if k < stages:
            for_both(1 << k, lambda peer: signal(ready_sem.at[k], (peer, xy)))

    def ready_wait(k):
        if k < stages:
            pl.semaphore_wait(ready_sem.at[k], beside(1 << k))

    def place(c):
        return c // per_field, pl.multiple_of(lax.rem(c, per_field) * ROWS, ROWS)

    def edge_copy(start, count):
        part = pl.ds(start, count)
        return pltpu.make_async_copy(fields_ref.at[:, part], inputs[0].at[:, part], edge_sem)

    def body_copy(c):
        f, row = place(c)
        where = (f, pl.ds(4, layers - 8), pl.ds(row, ROWS))
        return pltpu.make_async_copy(
            fields_ref.at[where], inputs[0].at[where], in_sem.at[c]
        )

    edge_copy(0, 4).start()
    edge_copy(layers - 4, 4).start()
    limit_copy = pltpu.make_async_copy(threshold_hbm, threshold_ref, limit_sem)
    limit_copy.start()

    @pl.loop(0, chunks)
    def _(c):
        body_copy(c).start()

    acc[...] = jnp.zeros_like(acc)

    def tiles(c):
        f, row = place(c)
        for t in range(ROWS // SUB):
            yield f, pl.ds(pl.multiple_of(row + t * SUB, SUB), SUB), pl.ds(t * SUB, SUB)

    def states_of(level, f, at, head):
        source = inputs[level]
        count = source.shape[1]
        make = head_states if head else tail_states
        return make(lambda j: source[f, j if j >= 0 else count + j, at])

    def put_states(buf, level, c, head):
        for f, at, to in tiles(c):
            one, two = states_of(level, f, at, head)
            buf[level, c, 0, to] = one
            buf[level, c, 1, to] = two

    units = LEVELS * chunks
    rows_between = gz_count // 4 - 1

    def by_relay(level, c, up, boundary):
        if up:
            share = (rows_between - boundary + 1) * units // (rows_between + 2)
        else:
            whole = 2 * (rows_between + 1) ** 2
            share = (2 * (boundary + 1) * (boundary + 1) * units + whole // 2 - 1) // whole
        unit = level * chunks + c
        return lax.rem(unit * share, units) < share

    def copy_of(send, recv, send_sem, recv_sem, level, c, peer):
        return pltpu.make_async_remote_copy(
            src_ref=send.at[level, c],
            dst_ref=recv.at[level, c],
            send_sem=send_sem,
            recv_sem=recv_sem,
            device_id={"gz": peer},
            device_id_type=MESH,
        )

    def lift(level, c, begin, end, low, high, emit_detail, emit_approx):
        source = inputs[level]
        half = source.shape[1] // 2
        final = level == LEVELS - 1
        limit = threshold_ref[c // per_field]

        def shrink(band):
            return band - jnp.minimum(jnp.maximum(band, -limit), limit)

        for f, at, to in tiles(c):
            evens = lambda i: source[f, 2 * i, at]
            odds = lambda i: source[f, 2 * i + 1, at]
            d1, s1, d2, sums = {}, {}, {}, {}

            def incoming(kind, which):
                if kind == "fast":
                    return fast_recv[level, c, which, to]
                if kind == "slow":
                    value = slow_recv[level, c, which, to]
                    return value + bias[c, which, to] if level else value
                return None

            def at_first(kind, mirrored, outer):
                return outer if kind == "fast" else jnp.where(first, mirrored, outer)

            def at_last(kind, mirrored, outer):
                outer = jnp.zeros_like(mirrored) if outer is None else outer
                return outer if kind == "fast" else jnp.where(last, mirrored, outer)

            def emit(kind, ref, i, value):
                band = shrink(value)
                ref[f, i, at] = band
                square = band * band
                sums[kind] = sums[kind] + square if kind in sums else square

            s = evens(begin)
            for i in range(begin, end + 1):
                if i < end:
                    if i + 1 < half:
                        s_next = evens(i + 1)
                    else:
                        s_next = at_last(high, s, incoming(high, 0))
                    d1[i] = odds(i) + ALPHA * (s + s_next)
                    if i == begin and low:
                        d1[i - 1] = at_first(low, d1[i], plus(incoming(low, 0), ALPHA * s))
                    if i - 1 in d1:
                        s1[i] = s + BETA * (d1[i - 1] + d1[i])
                    if i == begin and low:
                        s1[i - 1] = plus(incoming(low, 1), BETA * d1[i - 1])
                        d2[i - 1] = d1[i - 1] + GAMMA * (s1[i - 1] + s1[i])
                    s = s_next
                elif high:
                    s1[i] = at_last(high, s1[i - 1], plus(incoming(high, 1), BETA * d1[i - 1]))
                if i > begin and i - 1 in s1 and i in s1:
                    d2[i - 1] = d1[i - 1] + GAMMA * (s1[i - 1] + s1[i])
                    if i - 1 == begin and low:
                        d2[i - 2] = at_first(low, d2[i - 1], d2[i - 2])
                    if i - 1 in emit_detail:
                        emit(level, outs[level], i - 1, d2[i - 1] * (KAPPA / SQRT_TWO))
                    if i - 1 in emit_approx:
                        s2 = s1[i - 1] + DELTA * (d2[i - 2] + d2[i - 1])
                        approx = s2 * (SQRT_TWO / KAPPA)
                        if final:
                            emit(LEVELS, outs[LEVELS], i - 1, approx)
                        else:
                            inputs[level + 1][f, i - 1, at] = approx
            for kind, total in sums.items():
                acc[f, kind] += total

    lane = lax.broadcasted_iota(jnp.int32, (1, 128), 1)

    def reduced(f, row, kinds):
        for b in kinds:
            total = jnp.sum(jnp.sum(acc[f, b], axis=0, keepdims=True), axis=1, keepdims=True)
            row = jnp.where(lane == b, total, row)
        return row

    def analyse(head):
        slow_peer, fast_peer = (gz - 1, gz + 1) if head else (gz + 1, gz - 1)
        has_slow = gz > 0 if head else gz < gz_count - 1
        slow_copy = lambda level, c: copy_of(
            slow_send, slow_recv, slow_send_sem, slow_recv_sem.at[level, c], level, c, slow_peer
        )
        fast_copy = lambda level, c: copy_of(
            fast_send, fast_recv, fast_send_sem, fast_recv_sem.at[level % 2, c], level, c, fast_peer
        )
        touched = HEAD_TOUCHED if head else TAIL_TOUCHED
        far = (TRAIL_TAIL if head else TRAIL_HEAD)[1:] + ((3,) if head else (4,))
        top = LEVELS - 2

        def ends(slow, fast):
            return (slow, fast) if head else (fast, slow)

        relay_copy = lambda level, c: copy_of(
            slow_send, relay_buf, slow_send_sem, relay_sem.at[level, c], level, c, partner
        )
        onward = gz + 4 if head else gz - 4
        onward_copy = lambda level, c: copy_of(
            relay_buf, slow_recv, relay_sem.at[level, c], slow_recv_sem.at[level, c], level, c, onward
        )
        turn = jnp.logical_and(corner, has_slow)
        passes = jnp.logical_and(corner, gz < gz_count - 4 if head else gz >= 4)
        row = gz // 4

        def slow_start(level, c):
            if not relay:

                @pl.when(has_slow)
                def _():
                    slow_copy(level, c).start()

                return
            turned = jnp.logical_and(turn, by_relay(level, c, not head, row - 1 if head else row))

            @pl.when(turned)
            def _():
                relay_copy(level, c).start()

            late = head and level >= LATE
            straight = jnp.logical_and(corner, has_slow) if late else has_slow

            @pl.when(jnp.logical_and(straight, jnp.logical_not(turned)))
            def _():
                slow_copy(level, c).start()

        def pass_on(level, c, act):
            if relay:
                passed = by_relay(level, c, head, row if head else row - 1)

                @pl.when(jnp.logical_and(passes, passed))
                def _():
                    act(level, c)

        def receive_and_send(level, c):
            relay_copy(level, c).wait_recv()
            onward_copy(level, c).start()

        def bulk(level, c):
            half = inputs[level].shape[1] // 2
            details, _ = touched[level]
            keep = range(max(details, 1), half - 2) if head else range(1, half - max(details, 2))
            lift(level, c, 0, half - 1, None, None, keep, range(2, half - 2))
            rim(level, c, head, "local", 0, 2)

        def rim(level, c, low_end, kind, details, approx):
            half = inputs[level].shape[1] // 2
            if low_end:
                lift(level, c, 0, approx + 1, kind, None, range(details), range(approx))
            else:
                begin = half - approx - 2
                span = lambda n: range(half - n, half)
                lift(level, c, begin, half, None, kind, span(details), span(approx))

        def fast_rim(level, c):
            if level < top:
                rim(level, c, not head, "fast", 2 if head else 1, 2)
            else:
                half = inputs[level].shape[1] // 2
                lift(level, c, 0, half, *ends("local", "fast"), range(0), range(half))

        def reach_back(level, c):
            count = (TRAIL_TAIL if head else TRAIL_HEAD)[level]
            for f, at, to in tiles(c):
                states = states_of(level, f, at, head)
                if head:
                    entry = lambda j: trail[c, -1 - j, to] if -count <= j < 0 else None
                else:
                    entry = lambda j: trail[c, j, to] if 0 <= j < count else None
                added = echo(entry, states, not head)
                keep = far[level]
                for n in range(keep):
                    trail[c, n, to] = added[-1 - n if head else n]
                after = lambda j: added[j] if (-1 - j if head else j) < keep else None
                one, two = (tail_states if head else head_states)(after)
                bias[c, 0, to] = one
                bias[c, 1, to] = two

        def settle(level, c):
            if level < top:
                rim(level, c, head, "slow", *touched[level])
            else:
                half = inputs[level].shape[1] // 2
                lift(level, c, 0, half, *ends("slow", "fast"), range(half), range(half))

        edge_copy(0, 8).wait()

        @pl.loop(0, chunks)
        def _(c):
            put_states(slow_send, 0, c, head)
            put_states(fast_send, 0, c, not head)

        limit_copy.wait()
        greeted = corner.astype(jnp.int32) if relay else 0
        pl.semaphore_wait(barrier, beside(1) + greeted + xy_count - 1)

        @pl.loop(0, chunks)
        def _(c):
            slow_start(0, c)
            fast_copy(0, c).start()

        ready_signal(0)

        @pl.loop(0, chunks)
        def _(c):
            body_copy(c).wait()
            bulk(0, c)
            put_states(slow_send, 1, c, head)
            slow_start(1, c)

        ready_wait(0)
        ready_signal(1)

        for level in range(top + 1):

            @pl.loop(0, chunks)
            def _(c):
                fast_copy(level, c).wait_recv()
                fast_rim(level, c)
                if level < top:
                    put_states(fast_send, level + 1, c, not head)
                    fast_copy(level + 1, c).start()
                if level + 1 < top:
                    bulk(level + 1, c)
                if level + 2 <= top:
                    put_states(slow_send, level + 2, c, head)
                    slow_start(level + 2, c)
                if level == top:
                    put_states(slow_send, top + 1, c, head)
                    slow_start(top + 1, c)

        if relay and head:

            @pl.when(jnp.logical_not(corner))
            def _():
                for level in range(LATE, LEVELS):

                    @pl.loop(0, chunks)
                    def _(c):
                        slow_copy(level, c).start()

        ready_wait(1)
        ready_signal(2)
        if relay:

            @pl.loop(0, chunks)
            def _(c):
                for level in range(AHEAD):
                    pass_on(level, c, receive_and_send)

        for level in range(top + 1):
            if level:
                ready_wait(level + 1)
                ready_signal(level + 2)

            @pl.loop(0, chunks)
            def _(c):
                if level + AHEAD < LEVELS:
                    pass_on(level + AHEAD, c, receive_and_send)

                @pl.when(has_slow)
                def _():
                    slow_copy(level, c).wait_recv()

                settle(level, c)
                reach_back(level, c)
                if level == top:
                    put_states(fast_send, top + 1, c, not head)
                    fast_copy(top + 1, c).start()

        for stage in range(top + 2, stages):
            ready_wait(stage)
            ready_signal(stage + 1)

        zero = jnp.zeros((1, 128), jnp.float32)
        for f in range(field_count):
            e_send_buf[pl.ds(f, 1), :] = reduced(f, zero, range(top + 1))

        @pl.loop(0, chunks)
        def _(c):
            fast_copy(top + 1, c).wait_recv()

            @pl.when(has_slow)
            def _():
                slow_copy(top + 1, c).wait_recv()

            lift(top + 1, c, 0, 2, *ends("slow", "fast"), range(2), range(2))

        return lambda level, c: pass_on(level, c, lambda *at: onward_copy(*at).wait_send())

    def energy_copy(peer):
        return pltpu.make_async_remote_copy(
            src_ref=e_send_buf,
            dst_ref=e_recv_buf.at[me],
            send_sem=e_send_sem,
            recv_sem=e_recv_sem,
            device_id=peer,
            device_id_type=MESH,
        )

    def send_energies():
        for f in range(field_count):
            row = e_send_buf[pl.ds(f, 1), :]
            e_send_buf[pl.ds(f, 1), :] = reduced(f, row, range(LEVELS - 1, LEVELS + 1))
        for_peers(lambda peer: energy_copy(peer).start())

    def whole(head):
        finish = analyse(head)
        send_energies()
        if relay:

            @pl.loop(0, chunks)
            def _(c):
                for level in range(LEVELS):
                    finish(level, c)

    @pl.when(even)
    def _():
        whole(True)

    @pl.when(jnp.logical_not(even))
    def _():
        whole(False)

    e_recv_buf[me] = e_send_buf[...]

    pltpu.make_async_copy(fast_send, fast_send, fast_send_sem).wait()

    @pl.when(jnp.where(even, gz > 0, gz < gz_count - 1))
    def _():
        pltpu.make_async_copy(slow_send, slow_send, slow_send_sem).wait()

    others = e_recv_buf.at[pl.ds(0, devices - 1)]
    pltpu.make_async_copy(others, others, e_recv_sem).wait()

    totals = jnp.sum(e_recv_buf[...], axis=0)
    cells = jnp.ones((1, 128), jnp.float32)
    for b in range(LEVELS + 1):
        shape = outs[b].shape
        cells = jnp.where(lane == b, float(shape[1] * shape[2] * shape[3] * devices), cells)
    energy_ref[...] = (totals / cells)[:, : LEVELS + 1]

    pltpu.make_async_copy(others, others, e_send_sem).wait()


def write_out(*refs):
    count = (len(refs) - 1) // 2
    sources, targets, sems = refs[:count], refs[count : 2 * count], refs[-1]
    copies = [
        pltpu.make_async_copy(source, target, sems.at[k])
        for k, (source, target) in enumerate(zip(sources, targets))
    ]
    for copy in copies:
        copy.start()
    for copy in copies:
        copy.wait()


def zigzag(mesh):
    line = [getattr(device, "coords", None) for device in mesh.devices[:, 0]]
    if len(line) % 4 or None in line:
        return False
    apart = lambda a, b: sum(abs(p - q) for p, q in zip(line[a], line[b]))
    return all(
        (apart(g, g + 1), apart(g, g - 3), apart(g - 3, g + 1), apart(g + 1, g + 4), apart(g + 4, g))
        == (2, 1, 1, 1, 1)
        for g in range(3, len(line) - 1, 4)
    )


def solution(mesh):
    relay = zigzag(mesh)
    gz_count, xy_count = mesh.shape["gz"], mesh.shape["xy"]
    devices = gz_count * xy_count

    def local(fields, threshold):
        field_count, layers, width, depth = fields.shape
        chunks = field_count * (width // ROWS)
        assert gz_count % 2 == 0 and layers >> (LEVELS - 2) == 8
        f32 = jnp.float32
        halves = [layers >> (level + 1) for level in range(LEVELS)]
        band_layers = halves + halves[-1:]
        vmem = pl.BlockSpec(memory_space=pltpu.VMEM)
        shapes = tuple(
            jax.ShapeDtypeStruct((field_count, n, width, depth), f32) for n in band_layers
        ) + (jax.ShapeDtypeStruct((field_count, LEVELS + 1), f32),)
        results = pl.pallas_call(
            functools.partial(kernel, gz_count, xy_count, relay),
            out_shape=tuple(pltpu.VMEM(shape.shape, shape.dtype) for shape in shapes),
            in_specs=[
                pl.BlockSpec(memory_space=pltpu.HBM),
                pl.BlockSpec(memory_space=pltpu.HBM),
            ],
            out_specs=(vmem,) * (LEVELS + 2),
            scratch_shapes=[
                pltpu.VMEM((field_count, n, width, depth), f32) for n in [layers] + halves[:-1]
            ]
            + [
                pltpu.VMEM((LEVELS, chunks, 2, ROWS, depth), f32),
                pltpu.VMEM((LEVELS, chunks, 2, ROWS, depth), f32),
                pltpu.VMEM((LEVELS, chunks, 2, ROWS, depth), f32),
                pltpu.VMEM((LEVELS, chunks, 2, ROWS, depth), f32),
                pltpu.VMEM((LEVELS, chunks, 2, ROWS, depth), f32),
                pltpu.VMEM((chunks, 2, ROWS, depth), f32),
                pltpu.VMEM((chunks, 4, ROWS, depth), f32),
                pltpu.VMEM((field_count, LEVELS + 1, SUB, depth), f32),
                pltpu.VMEM((field_count, 128), f32),
                pltpu.VMEM((devices, field_count, 128), f32),
                pltpu.SMEM((field_count,), f32),
                pltpu.SemaphoreType.DMA((chunks,)),
                pltpu.SemaphoreType.DMA,
                pltpu.SemaphoreType.DMA,
                pltpu.SemaphoreType.DMA((LEVELS, chunks)),
                pltpu.SemaphoreType.DMA,
                pltpu.SemaphoreType.DMA((2, chunks)),
                pltpu.SemaphoreType.DMA((LEVELS, chunks)),
                pltpu.SemaphoreType.DMA,
                pltpu.SemaphoreType.DMA,
                pltpu.SemaphoreType.DMA,
                pltpu.SemaphoreType.REGULAR(((gz_count - 1).bit_length(),)),
            ],
            compiler_params=pltpu.CompilerParams(
                collective_id=0,
                has_side_effects=True,
                vmem_limit_bytes=32 * 1024 * 1024,
            ),
        )(
            pltpu.with_memory_space_constraint(threshold, pltpu.HBM),
            pltpu.with_memory_space_constraint(fields, pltpu.HBM),
        )
        return pl.pallas_call(
            write_out,
            out_shape=shapes,
            in_specs=[vmem] * (LEVELS + 2),
            out_specs=(pl.BlockSpec(memory_space=pltpu.HBM),) * (LEVELS + 2),
            scratch_shapes=[pltpu.SemaphoreType.DMA((LEVELS + 2,))],
            compiler_params=pltpu.CompilerParams(vmem_limit_bytes=4 * 1024 * 1024),
        )(*(pltpu.with_memory_space_constraint(result, pltpu.VMEM) for result in results))

    banded = P(None, "gz", "xy", None)
    return jax.shard_map(
        local,
        mesh=mesh,
        in_specs=(banded, P()),
        out_specs=(banded,) * (LEVELS + 1) + (P(),),
        check_vma=False,
    )
```
